32 devices in a mesh: groups: 2 (over x), rows: 16 (over z, y, core).
Axes of the slice: x: 2, y: 2, z: 4, core: 2. Of those that a mesh axis runs over, the one named last changes fastest.
Arguments:
- row_leaves: int32 [32, 65536], P(None, ('groups', 'rows')), parts along dimension 1, may hold values from 0 to 127
- covariates: bfloat16 [64, 65536], P(None, ('groups', 'rows')), parts along dimension 1, may hold values from -6 to 6
- query_leaves: int32 [32, 128], P(None, 'groups'), parts along dimension 1, may hold values from 0 to 127
- leaf_sizes: int32 [64, 128], P('groups'), parts along dimension 0, may hold values from 128 to 511
Outputs:
- moments: float32 [128, 4096], P(('groups', 'rows')), parts along dimension 0
The draws below stay inside these ranges and needn't reach their ends.
There are 2 independent parts, one for each index of `groups`. The reference program is written for one: setup_inputs(seed, part) draws one part's arguments, and reference() takes and returns one part's arrays. A program takes and returns all parts, laid end to end along the dimension named above; each array names one. Nothing has to cross between parts.
All inputs are finite; a program needn't handle non-finite values.
Results may differ from the reference program's by a relative error of at most 0.0006.
Values may be sent and summed in bfloat16 or wider, within the bound.
A program may use at most 64 MiB of HBM per device.

```python
import math
import jax
import jax.numpy as jnp
import numpy as np
from jax import lax

P_SIZE = 64
LEAVES = 128
TREES = 32
ROWS = 32768
Q = 64


def touch_ends(drawn, stream_key, least, high):
    longest = drawn.shape.index(max(drawn.shape))
    spots = []
    for shift in (0, 1):
        where = [jax.random.randint(jax.random.fold_in(stream_key, axis), (), 0, length) for axis, length in enumerate(drawn.shape)]
        where[longest] = (where[longest] + shift) % drawn.shape[longest]
        spots.append(tuple(where))
    return drawn.at[spots[0]].set(least).at[spots[1]].set(high)


def level_of(rng, dims, shards, low, largest):
    loudness = 1.0
    for dim, blocks in shards:
        heights = jax.random.uniform(jax.random.fold_in(jax.random.fold_in(rng, 6), dim), (blocks,), jnp.float32, low / len(shards), largest / len(shards))
        loudness = loudness * jnp.repeat(jnp.exp(heights), dims[dim] // blocks).reshape((-1,) + (1,) * (len(dims) - 1 - dim))
    return loudness


def cumulative_ranks(amount, slope):
    portions = [(1 << 20) // math.isqrt(grade ** slope) + 1 for grade in range(1, amount + 1)]
    width = 1 + sum(portions) // (1 << 30)
    return np.cumsum(np.array([max(1, weight // width) for weight in portions]))


def skewed_ids(own_key, shape, number_of, lean):
    listing = cumulative_ranks(number_of, lean)
    pick = jax.random.randint(jax.random.fold_in(own_key, 1), shape, 0, int(listing[number_of - 1]))
    standing = jnp.searchsorted(jnp.asarray(listing, jnp.int32), pick, side="right")
    return jax.random.permutation(jax.random.fold_in(own_key, 2), number_of)[standing].astype(jnp.int32)


def normal_values(own_key, shape, scale, reach, shards=(), held_as=jnp.bfloat16):
    entries = scale * jax.random.normal(own_key, shape, jnp.float32)
    if shards:
        entries = entries * level_of(own_key, shape, shards, -0.22, 0.18)
    return jnp.clip(entries, -reach, reach).astype(held_as)


def setup_inputs(seed: int = 0, part: int = 0) -> dict:
    splits = jax.random.split(jax.random.key(seed), 5)
    part_splits = jax.random.split(jax.random.fold_in(splits[4], part), 5)
    return {
        "row_leaves": touch_ends(jax.random.randint(part_splits[0], (TREES, ROWS), 0, LEAVES), jax.random.fold_in(part_splits[0], 1), 0, LEAVES - 1).astype(jnp.int32),
        "covariates": normal_values(part_splits[1], (P_SIZE, ROWS), 1.0, 6.0, ((1, 16),)),
        "query_leaves": touch_ends(skewed_ids(part_splits[2], (TREES, Q), LEAVES, 2), jax.random.fold_in(part_splits[2], 3), 0, LEAVES - 1).astype(jnp.int32),
        "leaf_sizes": touch_ends(jax.random.randint(part_splits[3], (TREES, LEAVES), ROWS // LEAVES // 2, 2 * ROWS // LEAVES), jax.random.fold_in(part_splits[3], 1), ROWS // LEAVES // 2, (2 * ROWS // LEAVES) - 1).astype(jnp.int32),
    }


def reference(row_leaves, covariates, query_leaves, leaf_sizes):
    inverse = 1.0 / (TREES * leaf_sizes.astype(jnp.float32))
    chosen = jnp.take_along_axis(inverse, query_leaves, axis=1).astype(jnp.bfloat16)
    chosen = lax.optimization_barrier(chosen).astype(jnp.float32)
    row_block = math.gcd(ROWS, 2048)
    count_blocks = ROWS // row_block
    leaf_blocks = jnp.transpose(row_leaves.reshape(TREES, count_blocks, row_block), (1, 0, 2))
    covar_blocks = jnp.transpose(covariates.reshape(P_SIZE, count_blocks, row_block), (1, 0, 2))

    def step(summed, inputs):
        leaf_block, covar_block = inputs
        match = query_leaves[:, :, None] == leaf_block[:, None, :]
        weights = jnp.sum(jnp.where(match, chosen[:, :, None], jnp.float32(0.0)), axis=0).astype(jnp.bfloat16)
        widened = covar_block.astype(jnp.float32)
        product = (widened[:, None, :] * widened[None, :, :]).reshape(P_SIZE * P_SIZE, row_block).astype(jnp.bfloat16)
        summed = summed + lax.dot_general(weights, product, (((1,), (1,)), ((), ())), preferred_element_type=jnp.float32)
        return summed, None

    summed, _ = lax.scan(step, jnp.zeros((Q, P_SIZE * P_SIZE), jnp.float32), (leaf_blocks, covar_blocks))
    return summed
```

```python
import functools

import jax
import jax.numpy as jnp
from jax import lax
from jax.experimental import pallas as pl
from jax.experimental.pallas import tpu as pltpu
from jax.sharding import PartitionSpec as P

CHUNKS = 2
SIDE = 16
LANES = 128
STEP = 256


def blocks_of(width):
    count = width // SIDE
    return [(a, b) for a in range(count) for b in range(a, count)]


def coded(value):
    largest = jnp.maximum(jnp.max(jnp.abs(value), axis=1, keepdims=True), 1e-30)
    power = jnp.floor(256.0 * jnp.log2(32000.0 / largest))
    whole = jnp.round(value * jnp.exp2(power * (1.0 / 256.0))).astype(jnp.int32)
    tail = jnp.broadcast_to(power.astype(jnp.int32), (value.shape[0], LANES))
    return jnp.concatenate([whole, tail], axis=1)


def decoded(code):
    wide = code.astype(jnp.int32).astype(jnp.float32)
    cols = wide.shape[1] - LANES
    return wide[:, :cols] * jnp.exp2(wide[:, cols:cols + 1] * (-1.0 / 256.0))


def kernel(n, rl_hbm, x_hbm, ql_hbm, ls_hbm, o_ref, rl, x, ql, ls, xf, qb, wb, w_s, prod, part, own, s3, r1, r3,
           late_sem, in_sems, rl_sems, ss1, rs1, ss3, rs3):
    trees, rows = rl.shape
    width = x.shape[0]
    queries = ql.shape[1]
    t = queries // n
    nz = n // 2
    half = nz // 2
    sub = nz * t
    per_chunk = len(blocks_of(width)) // CHUNKS
    me = lax.axis_index("rows")
    core = lax.rem(me, 2)
    z = me // 2
    tier = z // half
    spot = lax.rem(z, half)
    sibling = me + 1 - 2 * core

    def device(chip):
        return chip * 2 + core

    def same_tier(d):
        return tier * half + lax.rem(spot + d, half)

    def other_tier(d):
        return (1 - tier) * half + lax.rem(spot + d, half)

    def greet(sem, peer):
        pl.semaphore_signal(sem, inc=1, device_id={"rows": peer}, device_id_type=pl.DeviceIdType.MESH)

    barrier = pltpu.get_barrier_semaphore()
    greet(barrier, sibling)
    for d in range(1, half):
        greet(barrier, device(same_tier(d)))

    @pl.when(tier == 0)
    def _():
        for d in range(half):
            greet(barrier, device(other_tier(d)))

    def rl_copy(step):
        at = pl.ds(pl.multiple_of(step * STEP, STEP), STEP)
        return pltpu.make_async_copy(rl_hbm.at[:, at], rl.at[:, at], rl_sems.at[step])

    ins = [pltpu.make_async_copy(a, b, in_sems.at[i])
           for i, (a, b) in enumerate(((ls_hbm, ls), (ql_hbm, ql), (x_hbm, x)))]
    ins[0].start()
    ins[1].start()
    for step in range(rows // STEP):
        rl_copy(step).start()
    ins[2].start()
    ins[0].wait()
    ins[1].wait()

    units = float(128 * trees * 2 * rows * n // ls.shape[1])
    inverse = 1.0 / (trees * ls[...].astype(jnp.float32))
    leaf_cols, weight_cols = [], []
    for first in range(0, queries, LANES):
        piece = ql[:, first:first + LANES]
        if piece.shape[1] < LANES:
            piece = jnp.concatenate([piece] * (LANES // piece.shape[1]), axis=1)
        chosen = jnp.take_along_axis(inverse, piece, axis=1).astype(jnp.bfloat16).astype(jnp.float32)
        leaf_cols.append(piece.T)
        weight_cols.append((chosen * units).astype(jnp.int32).T)

    def ordered(cols_list):
        out = []
        for c in range(2):
            for k in range(nz):
                first = (k * 2 + c) * t
                out.append(cols_list[first // LANES][first % LANES:first % LANES + t])
        return jnp.concatenate(out, axis=0)

    leaf_t = ordered(leaf_cols)
    weight_t = ordered(weight_cols)
    for b in range(trees):
        qb[b] = jnp.broadcast_to(leaf_t[:, b:b + 1], (queries, STEP)).astype(jnp.int16)
        wb[b] = jnp.broadcast_to(weight_t[:, b:b + 1], (queries, STEP)).astype(jnp.int16)

    tile = 64
    share = 8

    def weights_step(step, carry):
        at = pl.ds(pl.multiple_of(step * STEP, STEP), STEP)
        rl_copy(step).wait()
        for q0 in range(0, queries, tile):
            def tree(b, acc):
                row = jnp.broadcast_to(rl[pl.ds(b, 1), at], (8, STEP)).astype(jnp.int16)
                row = jnp.concatenate([row] * (tile // 8), axis=0)
                weight = wb[b, q0:q0 + tile, :]
                return acc + jnp.where(qb[b, q0:q0 + tile, :] == row, weight, jnp.zeros_like(weight))

            acc = lax.fori_loop(0, trees, tree, jnp.zeros((tile, STEP), jnp.int16), unroll=share)
            total = acc.astype(jnp.int32).astype(jnp.float32) * (1.0 / units)
            w_s[q0:q0 + tile, at] = total.astype(jnp.bfloat16)
        return carry

    lax.fori_loop(0, rows // STEP, weights_step, 0)
    ins[2].wait()
    xf[...] = x[...].astype(jnp.float32)

    blocks = blocks_of(width)
    area = SIDE * SIDE

    def compute(c):
        for g in range(per_chunk):
            first, second = blocks[c * per_chunk + g]
            right = x[second * SIDE:(second + 1) * SIDE, :]
            for jj in range(SIDE):
                j = first * SIDE + jj
                xb = jnp.broadcast_to(xf[j:j + 1, :], (SIDE, rows)).astype(jnp.bfloat16)
                prod[g % 2, jj * SIDE:(jj + 1) * SIDE, :] = right * xb
            res = lax.dot_general(w_s[...], prod[g % 2], (((1,), (1,)), ((), ())),
                                  preferred_element_type=jnp.float32)
            for a in range(2):
                part[c, a, :, g * area:(g + 1) * area] = res[a * sub:(a + 1) * sub, :]

    def copy(src, dst, ssem, rsem, peer):
        return pltpu.make_async_remote_copy(src_ref=src, dst_ref=dst, send_sem=ssem, recv_sem=rsem,
                                            device_id={"rows": peer}, device_id_type=pl.DeviceIdType.MESH)

    def c1(c):
        return copy(part.at[c, 1 - core], r1.at[c], ss1.at[c], rs1.at[c], sibling)

    def c3(c, chip):
        return copy(s3.at[c, chip], r3.at[c, z], ss3.at[c, chip], rs3.at[c, z], device(chip))

    def r3_wait(c, chip):
        copy(s3.at[c, chip], r3.at[c, chip], ss3.at[c, chip], rs3.at[c, chip], device(chip)).wait_recv()

    def encode(c):
        c1(c).wait_recv()
        total = part[c, core] + r1[c]
        code = coded(total)
        for k in range(nz):
            own[c, k] = total[k * t:(k + 1) * t, :]
            s3[c, k] = code[k * t:(k + 1) * t, :].astype(jnp.int16)

    def send_same(c):
        for d in range(1, half):
            c3(c, same_tier(d)).start()

    def send_other(c):
        for d in range(half):
            c3(c, other_tier(d)).start()

    @pl.when(tier == 1)
    def _():
        pl.semaphore_wait(barrier, nz)
        for d in range(half):
            greet(late_sem, device(other_tier(d)))

    compute(0)

    @pl.when(tier == 0)
    def _():
        pl.semaphore_wait(barrier, half)

    c1(0).start()
    for c in range(CHUNKS):
        if c + 1 < CHUNKS:
            compute(c + 1)
            c1(c + 1).start()
        encode(c)

        @pl.when(tier == 0)
        def _():
            send_same(c)

        @pl.when(tier == 1)
        def _():
            send_other(c)
            send_same(c)

    @pl.when(tier == 0)
    def _():
        pl.semaphore_wait(late_sem, half)
        for c in range(CHUNKS):
            send_other(c)

    for c in range(CHUNKS):
        total = own[c, z]
        for d in range(1, nz):
            chip = lax.rem(z + d, nz)
            r3_wait(c, chip)
            total = total + decoded(r3[c, chip])
        o_ref[:, c * per_chunk * area:(c + 1) * per_chunk * area] = total
    for c in range(CHUNKS):
        c1(c).wait_send()
        for d in range(1, nz):
            c3(c, lax.rem(z + d, nz)).wait_send()


def unfold(width, v_ref, o_ref, grid, turn):
    t = v_ref.shape[0]
    count = width // SIDE
    area = SIDE * SIDE
    blocks = blocks_of(width)
    upper = [(a, b) for a, b in blocks if a != b]
    for g, (a, b) in enumerate(blocks):
        block = v_ref[:, g * area:(g + 1) * area]
        grid[b, a * t:(a + 1) * t, :] = block
        if a != b:
            at = upper.index((a, b)) * t
            turn[at:at + t, :] = block
    value = turn[...]
    source = lax.broadcasted_iota(jnp.int32, (area, area), 0)
    target = lax.broadcasted_iota(jnp.int32, (area, area), 1)
    swap = jnp.where(source == lax.rem(target, SIDE) * SIDE + target // SIDE, 1.0, 0.0).astype(jnp.bfloat16)
    turned = jnp.zeros(value.shape, jnp.float32)
    for _ in range(3):
        piece = value.astype(jnp.bfloat16)
        turned = turned + jnp.dot(piece, swap, preferred_element_type=jnp.float32)
        value = value - piece.astype(jnp.float32)
    for i, (a, b) in enumerate(upper):
        grid[a, b * t:(b + 1) * t, :] = turned[i * t:(i + 1) * t, :]
    lane = lax.broadcasted_iota(jnp.int32, (count * t, LANES), 1)
    group = lax.rem(lane, width) // SIDE
    for tile_at in range(SIDE * width // LANES):
        per_tile = LANES // width
        src = tile_at * per_tile * SIDE
        pick = src % LANES + lane // width * SIDE + lax.rem(lane, SIDE)
        base = src // LANES * LANES
        out = jnp.zeros((count * t, LANES), jnp.float32)
        for b in range(count):
            out = jnp.where(group == b, jnp.take_along_axis(grid[b, :, base:base + LANES], pick, axis=1), out)
        for a in range(count):
            at = a * SIDE * width + tile_at * LANES
            o_ref[:, at:at + LANES] = out[a * t:(a + 1) * t, :]


def per_device(row_leaves, covariates, query_leaves, leaf_sizes):
    n = lax.axis_size("rows")
    trees, rows = row_leaves.shape
    width = covariates.shape[0]
    queries = query_leaves.shape[1]
    t = queries // n
    nz = n // 2
    sub = nz * t
    per_chunk = len(blocks_of(width)) // CHUNKS
    cols = per_chunk * SIDE * SIDE
    count = width // SIDE
    vmem = pl.BlockSpec(memory_space=pltpu.VMEM)
    f32 = jnp.float32
    i16 = jnp.int16
    dma = pltpu.SemaphoreType.DMA
    folded = pl.pallas_call(
        functools.partial(kernel, n),
        out_shape=pltpu.VMEM((t, CHUNKS * cols), f32),
        in_specs=[pl.BlockSpec(memory_space=pltpu.HBM)] * 4,
        out_specs=vmem,
        scratch_shapes=[
            pltpu.VMEM(row_leaves.shape, jnp.int32),
            pltpu.VMEM(covariates.shape, jnp.bfloat16),
            pltpu.VMEM(query_leaves.shape, jnp.int32),
            pltpu.VMEM(leaf_sizes.shape, jnp.int32),
            pltpu.VMEM((width, rows), f32),
            pltpu.VMEM((trees, queries, STEP), i16),
            pltpu.VMEM((trees, queries, STEP), i16),
            pltpu.VMEM((queries, rows), jnp.bfloat16),
            pltpu.VMEM((2, SIDE * SIDE, rows), jnp.bfloat16),
            pltpu.VMEM((CHUNKS, 2, sub, cols), f32),
            pltpu.VMEM((CHUNKS, nz, t, cols), f32),
            pltpu.VMEM((CHUNKS, nz, t, cols + LANES), i16),
            pltpu.VMEM((CHUNKS, sub, cols), f32),
            pltpu.VMEM((CHUNKS, nz, t, cols + LANES), i16),
            pltpu.SemaphoreType.REGULAR,
            dma((3,)), dma((rows // STEP,)),
            dma((CHUNKS,)), dma((CHUNKS,)),
            dma((CHUNKS, nz)), dma((CHUNKS, nz)),
        ],
        compiler_params=pltpu.CompilerParams(collective_id=0, has_side_effects=True,
                                             vmem_limit_bytes=56 << 20),
    )(row_leaves, covariates, query_leaves, leaf_sizes)
    return pl.pallas_call(
        functools.partial(unfold, width),
        out_shape=jax.ShapeDtypeStruct((t, width * width), f32),
        in_specs=[vmem],
        out_specs=vmem,
        scratch_shapes=[
            pltpu.VMEM((count, count * t, SIDE * SIDE), f32),
            pltpu.VMEM((count * (count - 1) // 2 * t, SIDE * SIDE), f32),
        ],
        compiler_params=pltpu.CompilerParams(vmem_limit_bytes=16 << 20),
    )(folded)


def solution(mesh):
    return jax.shard_map(
        per_device,
        mesh=mesh,
        in_specs=(
            P(None, ("groups", "rows")),
            P(None, ("groups", "rows")),
            P(None, "groups"),
            P("groups", None),
        ),
        out_specs=P(("groups", "rows"), None),
        check_vma=False,
    )
```

```python
import functools

import jax
import jax.numpy as jnp
from jax import lax
from jax.experimental import pallas as pl
from jax.experimental.pallas import tpu as pltpu
from jax.sharding import PartitionSpec as P

LANES = 128
STEP = 256
TURNS = 8


def splits_of(width):
    return [(0, width // 4), (width // 4, width // 2 + 1)]


def coded(value):
    largest = jnp.maximum(jnp.max(jnp.abs(value), axis=1, keepdims=True), 1e-30)
    power = jnp.floor(256.0 * jnp.log2(32000.0 / largest))
    whole = jnp.round(value * jnp.exp2(power * (1.0 / 256.0))).astype(jnp.int32)
    spare = -value.shape[1] % LANES or LANES
    tail = jnp.broadcast_to(power.astype(jnp.int32), (value.shape[0], spare))
    return jnp.concatenate([whole, tail], axis=1)


def coded_width(cols):
    return cols + (-cols % LANES or LANES)


def decoded(code, cols):
    wide = code.astype(jnp.int32).astype(jnp.float32)
    return wide[:, :cols] * jnp.exp2(wide[:, cols:cols + 1] * (-1.0 / 256.0))


def kernel(n, rl_hbm, x_hbm, ql_hbm, ls_hbm, o_ref, rl, x, ql, ls, turns, qb, wb, w_s, late_sem, in_sems, rl_sems,
           ss1, rs1, ss3, rs3, *bufs):
    trees, rows = rl.shape
    width = x.shape[0]
    queries = ql.shape[1]
    splits = splits_of(width)
    chunks = len(splits)
    part, own, s3, r1, r3 = (bufs[i * chunks:(i + 1) * chunks] for i in range(5))
    t = queries // n
    nz = n // 2
    half = nz // 2
    sub = nz * t
    me = lax.axis_index("rows")
    core = lax.rem(me, 2)
    z = me // 2
    tier = z // half
    spot = lax.rem(z, half)
    sibling = me + 1 - 2 * core

    def device(chip):
        return chip * 2 + core

    def same_tier(d):
        return tier * half + lax.rem(spot + d, half)

    def other_tier(d):
        return (1 - tier) * half + lax.rem(spot + d, half)

    def greet(sem, peer):
        pl.semaphore_signal(sem, inc=1, device_id={"rows": peer}, device_id_type=pl.DeviceIdType.MESH)

    barrier = pltpu.get_barrier_semaphore()
    greet(barrier, sibling)
    for d in range(1, half):
        greet(barrier, device(same_tier(d)))

    @pl.when(tier == 0)
    def _():
        for d in range(half):
            greet(barrier, device(other_tier(d)))

    def rl_copy(step):
        at = pl.ds(pl.multiple_of(step * STEP, STEP), STEP)
        return pltpu.make_async_copy(rl_hbm.at[:, at], rl.at[:, at], rl_sems.at[step])

    ins = [pltpu.make_async_copy(a, b, in_sems.at[i])
           for i, (a, b) in enumerate(((ls_hbm, ls), (ql_hbm, ql), (x_hbm, x)))]
    ins[0].start()
    ins[1].start()
    for step in range(rows // STEP):
        rl_copy(step).start()
    ins[2].start()
    ins[0].wait()
    ins[1].wait()

    bf16 = jnp.bfloat16
    units = float(128 * trees * 2 * rows * n // ls.shape[1])
    inverse = 1.0 / (trees * ls[...].astype(jnp.float32))
    chosen = []
    for first in range(0, queries, LANES):
        piece = ql[:, first:first + LANES]
        wide = piece.shape[1]
        if wide < LANES:
            piece = jnp.concatenate([piece] * (LANES // wide), axis=1)
        chosen.append(jnp.take_along_axis(inverse, piece, axis=1)[:, :wide])
    chosen = jnp.concatenate(chosen, axis=1).astype(bf16) * bf16(units)
    place = lax.broadcasted_iota(jnp.int32, (queries, queries), 0)
    query = lax.broadcasted_iota(jnp.int32, (queries, queries), 1)
    pick = (lax.rem(place, sub) // t * 2 + place // sub) * t + lax.rem(place, t)
    order = jnp.where(query == pick, 1.0, 0.0).astype(bf16)
    tree_of = lax.broadcasted_iota(jnp.int32, (trees, trees * LANES), 1) // LANES
    spread = jnp.where(tree_of == lax.broadcasted_iota(jnp.int32, (trees, trees * LANES), 0), 1.0, 0.0).astype(bf16)
    for table, out in ((ql[...].astype(jnp.float32).astype(bf16), qb), (chosen, wb)):
        sorted_t = lax.dot_general(order, table, (((1,), (1,)), ((), ())), preferred_element_type=jnp.float32)
        wide = jnp.dot(sorted_t.astype(bf16), spread, preferred_element_type=jnp.float32).astype(jnp.int32)
        for b in range(trees):
            one = wide[:, b * LANES:(b + 1) * LANES]
            out[b] = jnp.concatenate([one] * (STEP // LANES), axis=1).astype(jnp.int16)

    tile = 64
    share = 8

    def weights_step(step, carry):
        at = pl.ds(pl.multiple_of(step * STEP, STEP), STEP)
        rl_copy(step).wait()
        for q0 in range(0, queries, tile):
            def tree(b, acc):
                row = jnp.broadcast_to(rl[pl.ds(b, 1), at], (8, STEP)).astype(jnp.int16)
                row = jnp.concatenate([row] * (tile // 8), axis=0)
                weight = wb[b, q0:q0 + tile, :]
                return acc + jnp.where(qb[b, q0:q0 + tile, :] == row, weight, jnp.zeros_like(weight))

            acc = lax.fori_loop(0, trees, tree, jnp.zeros((tile, STEP), jnp.int16), unroll=share)
            total = acc.astype(jnp.int32).astype(jnp.float32) * (1.0 / units)
            w_s[q0:q0 + tile, at] = total.astype(jnp.bfloat16)
        return carry

    lax.fori_loop(0, rows // STEP, weights_step, 0)
    ins[2].wait()
    for at in range(0, rows, 2 * STEP):
        wide = x[:, at:at + 2 * STEP].astype(jnp.float32)
        for r in range(TURNS):
            turned = (jnp.roll(wide, -r, axis=0) if r else wide).astype(bf16)
            turns[r, :width, at:at + 2 * STEP] = turned
            turns[r, width:, at:at + 2 * STEP] = turned[:turns.shape[1] - width]

    def compute(c):
        lo, hi = splits[c]
        per = STEP // width
        for s in range(lo, hi, per):
            ends = min(hi, s + per)
            prod = jnp.concatenate(
                [x[...] * turns[e % TURNS, e // TURNS * TURNS:e // TURNS * TURNS + width, :] for e in range(s, ends)], axis=0)
            res = lax.dot_general(w_s[...], prod, (((1,), (1,)), ((), ())), preferred_element_type=jnp.float32)
            for a in range(2):
                part[c][a, :, (s - lo) * width:(ends - lo) * width] = res[a * sub:(a + 1) * sub, :]

    def copy(src, dst, ssem, rsem, peer):
        return pltpu.make_async_remote_copy(src_ref=src, dst_ref=dst, send_sem=ssem, recv_sem=rsem,
                                            device_id={"rows": peer}, device_id_type=pl.DeviceIdType.MESH)

    def c1(c):
        return copy(part[c].at[1 - core], r1[c], ss1.at[c], rs1.at[c], sibling)

    def c3(c, chip):
        return copy(s3[c].at[chip], r3[c].at[z], ss3.at[c, chip], rs3.at[c, z], device(chip))

    def r3_wait(c, chip):
        copy(s3[c].at[chip], r3[c].at[chip], ss3.at[c, chip], rs3.at[c, chip], device(chip)).wait_recv()

    def encode(c):
        c1(c).wait_recv()
        total = part[c][core] + r1[c][...]
        code = coded(total)
        for k in range(nz):
            own[c][k] = total[k * t:(k + 1) * t, :]
            s3[c][k] = code[k * t:(k + 1) * t, :].astype(jnp.int16)

    def send_same(c):
        for d in range(1, half):
            c3(c, same_tier(d)).start()

    def send_other(c):
        for d in range(half):
            c3(c, other_tier(d)).start()

    @pl.when(tier == 1)
    def _():
        pl.semaphore_wait(barrier, nz)
        for d in range(half):
            greet(late_sem, device(other_tier(d)))

    compute(0)

    @pl.when(tier == 0)
    def _():
        pl.semaphore_wait(barrier, half)

    c1(0).start()
    for c in range(chunks):
        if c + 1 < chunks:
            compute(c + 1)
            c1(c + 1).start()
        encode(c)

        @pl.when(tier == 0)
        def _():
            send_same(c)

        @pl.when(tier == 1)
        def _():
            send_other(c)
            send_same(c)

    @pl.when(tier == 0)
    def _():
        pl.semaphore_wait(late_sem, half)
        for c in range(chunks):
            send_other(c)

    for c in range(chunks):
        lo, hi = splits[c]
        total = own[c][z]
        for d in range(1, nz):
            chip = lax.rem(z + d, nz)
            r3_wait(c, chip)
            total = total + decoded(r3[c][chip], (hi - lo) * width)
        for s in range(lo, hi):
            o_ref[s * t:(s + 1) * t, :] = total[:, (s - lo) * width:(s - lo + 1) * width]
    for c in range(chunks):
        c1(c).wait_send()
        for d in range(1, nz):
            c3(c, lax.rem(z + d, nz)).wait_send()


def unfold(t, v_ref, o_ref, lined):
    width = v_ref.shape[1]
    far = width // 2
    value = jnp.concatenate([v_ref[...], jnp.zeros((width * t - v_ref.shape[0], width), jnp.float32)], axis=0)
    lane = lax.broadcasted_iota(jnp.int32, value.shape, 1)
    step = 1
    while step < width:
        value = jnp.where((lane & step) != 0, jnp.roll(value, step * t, axis=0), value)
        step *= 2
    lined[...] = value
    row = lax.broadcasted_iota(jnp.int32, (width, width), 0)
    col = lax.broadcasted_iota(jnp.int32, (width, width), 1)
    near = lax.rem(row - col + width, width) <= far
    for q in range(t):
        at = pl.ds(q, width, stride=t)
        below = lined[at, :]
        lined[at, :] = jnp.where(near, below, below.T)
    per = LANES // width
    for m in range(width // per):
        o_ref[:, m * LANES:(m + 1) * LANES] = jnp.concatenate(
            [lined[(m * per + i) * t:(m * per + i + 1) * t, :] for i in range(per)], axis=1)


def per_device(row_leaves, covariates, query_leaves, leaf_sizes):
    n = lax.axis_size("rows")
    trees, rows = row_leaves.shape
    width = covariates.shape[0]
    queries = query_leaves.shape[1]
    t = queries // n
    nz = n // 2
    sub = nz * t
    cols = [(hi - lo) * width for lo, hi in splits_of(width)]
    chunks = len(cols)
    vmem = pl.BlockSpec(memory_space=pltpu.VMEM)
    f32 = jnp.float32
    i16 = jnp.int16
    dma = pltpu.SemaphoreType.DMA
    folded = pl.pallas_call(
        functools.partial(kernel, n),
        out_shape=pltpu.VMEM(((width // 2 + 1) * t, width), f32),
        in_specs=[pl.BlockSpec(memory_space=pltpu.HBM)] * 4,
        out_specs=vmem,
        scratch_shapes=[
            pltpu.VMEM(row_leaves.shape, jnp.int32),
            pltpu.VMEM(covariates.shape, jnp.bfloat16),
            pltpu.VMEM(query_leaves.shape, jnp.int32),
            pltpu.VMEM(leaf_sizes.shape, jnp.int32),
            pltpu.VMEM((TURNS, width + width // 2, rows), jnp.bfloat16),
            pltpu.VMEM((trees, queries, STEP), i16),
            pltpu.VMEM((trees, queries, STEP), i16),
            pltpu.VMEM((queries, rows), jnp.bfloat16),
            pltpu.SemaphoreType.REGULAR,
            dma((3,)), dma((rows // STEP,)),
            dma((chunks,)), dma((chunks,)),
            dma((chunks, nz)), dma((chunks, nz)),
            *[pltpu.VMEM((2, sub, c), f32) for c in cols],
            *[pltpu.VMEM((nz, t, c), f32) for c in cols],
            *[pltpu.VMEM((nz, t, coded_width(c)), i16) for c in cols],
            *[pltpu.VMEM((sub, c), f32) for c in cols],
            *[pltpu.VMEM((nz, t, coded_width(c)), i16) for c in cols],
        ],
        compiler_params=pltpu.CompilerParams(collective_id=0, has_side_effects=True,
                                             vmem_limit_bytes=56 << 20),
    )(row_leaves, covariates, query_leaves, leaf_sizes)
    return pl.pallas_call(
        functools.partial(unfold, t),
        out_shape=jax.ShapeDtypeStruct((t, width * width), f32),
        in_specs=[vmem],
        out_specs=vmem,
        scratch_shapes=[pltpu.VMEM((width * t, width), f32)],
        compiler_params=pltpu.CompilerParams(vmem_limit_bytes=16 << 20),
    )(folded)


def solution(mesh):
    return jax.shard_map(
        per_device,
        mesh=mesh,
        in_specs=(
            P(None, ("groups", "rows")),
            P(None, ("groups", "rows")),
            P(None, "groups"),
            P("groups", None),
        ),
        out_specs=P(("groups", "rows"), None),
        check_vma=False,
    )
```

```python
import functools

import jax
import jax.numpy as jnp
from jax import lax
from jax.experimental import pallas as pl
from jax.experimental.pallas import tpu as pltpu
from jax.sharding import PartitionSpec as P

LANES = 128
STEP = 256
TURNS = 8


def splits_of(width):
    return [(0, width // 4), (width // 4, width // 2 + 1)]


def coded(value):
    largest = jnp.maximum(jnp.max(jnp.abs(value), axis=1, keepdims=True), 1e-30)
    power = jnp.floor(256.0 * jnp.log2(32000.0 / largest))
    whole = jnp.round(value * jnp.exp2(power * (1.0 / 256.0))).astype(jnp.int32)
    spare = -value.shape[1] % LANES or LANES
    tail = jnp.broadcast_to(power.astype(jnp.int32), (value.shape[0], spare))
    return jnp.concatenate([whole, tail], axis=1)


def coded_width(cols):
    return cols + (-cols % LANES or LANES)


def decoded(code, cols):
    wide = code.astype(jnp.int32).astype(jnp.float32)
    return wide[:, :cols] * jnp.exp2(wide[:, cols:cols + 1] * (-1.0 / 256.0))


def kernel(n, rl_hbm, x_hbm, ql_hbm, ls_hbm, o_ref, rl, x, ql, ls, turns, qb, wb, w_s, order, spread, late_sem, in_sems, rl_sems,
           ss1, rs1, ss3, rs3, *bufs):
    trees, rows = rl.shape
    width = x.shape[0]
    queries = ql.shape[1]
    splits = splits_of(width)
    chunks = len(splits)
    part, own, s3, r1, r3 = (bufs[i * chunks:(i + 1) * chunks] for i in range(5))
    t = queries // n
    nz = n // 2
    half = nz // 2
    sub = nz * t
    me = lax.axis_index("rows")
    core = lax.rem(me, 2)
    z = me // 2
    tier = z // half
    spot = lax.rem(z, half)
    sibling = me + 1 - 2 * core

    def device(chip):
        return chip * 2 + core

    def same_tier(d):
        return tier * half + lax.rem(spot + d, half)

    def other_tier(d):
        return (1 - tier) * half + lax.rem(spot + d, half)

    def greet(sem, peer):
        pl.semaphore_signal(sem, inc=1, device_id={"rows": peer}, device_id_type=pl.DeviceIdType.MESH)

    def rl_copy(step):
        at = pl.ds(pl.multiple_of(step * STEP, STEP), STEP)
        return pltpu.make_async_copy(rl_hbm.at[:, at], rl.at[:, at], rl_sems.at[step])

    ins = [pltpu.make_async_copy(a, b, in_sems.at[i])
           for i, (a, b) in enumerate(((ls_hbm, ls), (ql_hbm, ql), (x_hbm, x)))]
    ins[0].start()
    ins[1].start()
    for step in range(rows // STEP):
        rl_copy(step).start()
    ins[2].start()

    barrier = pltpu.get_barrier_semaphore()
    greet(barrier, sibling)
    for d in range(1, half):
        greet(barrier, device(same_tier(d)))

    @pl.when(tier == 0)
    def _():
        for d in range(half):
            greet(barrier, device(other_tier(d)))

    bf16 = jnp.bfloat16
    place = lax.broadcasted_iota(jnp.int32, (queries, queries), 0)
    query = lax.broadcasted_iota(jnp.int32, (queries, queries), 1)
    pick = (lax.rem(place, sub) // t * 2 + place // sub) * t + lax.rem(place, t)
    order[...] = jnp.where(query == pick, 1.0, 0.0).astype(bf16)
    tree_of = lax.broadcasted_iota(jnp.int32, (trees, trees * LANES), 1) // LANES
    tree_at = lax.broadcasted_iota(jnp.int32, (trees, trees * LANES), 0)
    spread[...] = jnp.where(tree_of == tree_at, 1.0, 0.0).astype(bf16)
    ins[0].wait()
    ins[1].wait()

    units = float(128 * trees * 2 * rows * n // ls.shape[1])
    inverse = 1.0 / (trees * ls[...].astype(jnp.float32))
    chosen = []
    for first in range(0, queries, LANES):
        piece = ql[:, first:first + LANES]
        wide = piece.shape[1]
        if wide < LANES:
            piece = jnp.concatenate([piece] * (LANES // wide), axis=1)
        chosen.append(jnp.take_along_axis(inverse, piece, axis=1)[:, :wide])
    chosen = jnp.concatenate(chosen, axis=1).astype(bf16) * bf16(units)
    for table, out in ((ql[...].astype(jnp.float32).astype(bf16), qb), (chosen, wb)):
        sorted_t = lax.dot_general(order[...], table, (((1,), (1,)), ((), ())), preferred_element_type=jnp.float32)
        wide = jnp.dot(sorted_t.astype(bf16), spread[...], preferred_element_type=jnp.float32).astype(jnp.int32)
        for b in range(trees):
            one = wide[:, b * LANES:(b + 1) * LANES]
            out[b] = jnp.concatenate([one] * (STEP // LANES), axis=1).astype(jnp.int16)

    tile = 64
    share = 8

    def weights_step(step, carry):
        at = pl.ds(pl.multiple_of(step * STEP, STEP), STEP)
        rl_copy(step).wait()
        for q0 in range(0, queries, tile):
            def tree(b, acc):
                row = jnp.broadcast_to(rl[pl.ds(b, 1), at], (8, STEP)).astype(jnp.int16)
                row = jnp.concatenate([row] * (tile // 8), axis=0)
                weight = wb[b, q0:q0 + tile, :]
                return acc + jnp.where(qb[b, q0:q0 + tile, :] == row, weight, jnp.zeros_like(weight))

            acc = lax.fori_loop(0, trees, tree, jnp.zeros((tile, STEP), jnp.int16), unroll=share)
            total = acc.astype(jnp.int32).astype(jnp.float32) * (1.0 / units)
            w_s[q0:q0 + tile, at] = total.astype(jnp.bfloat16)
        return carry

    lax.fori_loop(0, rows // STEP, weights_step, 0)
    ins[2].wait()
    def turn():
        for at in range(0, rows, 2 * STEP):
            wide = x[:, at:at + 2 * STEP].astype(jnp.float32)
            for r in range(TURNS):
                turned = (jnp.roll(wide, -r, axis=0) if r else wide).astype(bf16)
                turns[r, :width, at:at + 2 * STEP] = turned
                turns[r, width:, at:at + 2 * STEP] = turned[:turns.shape[1] - width]

    def compute(c):
        lo, hi = splits[c]
        per = STEP // width
        for s in range(lo, hi, per):
            ends = min(hi, s + per)
            prod = jnp.concatenate(
                [x[...] * turns[e % TURNS, e // TURNS * TURNS:e // TURNS * TURNS + width, :] for e in range(s, ends)], axis=0)
            res = lax.dot_general(w_s[...], prod, (((1,), (1,)), ((), ())), preferred_element_type=jnp.float32)
            for a in range(2):
                part[c][a, :, (s - lo) * width:(ends - lo) * width] = res[a * sub:(a + 1) * sub, :]

    def copy(src, dst, ssem, rsem, peer):
        return pltpu.make_async_remote_copy(src_ref=src, dst_ref=dst, send_sem=ssem, recv_sem=rsem,
                                            device_id={"rows": peer}, device_id_type=pl.DeviceIdType.MESH)

    def c1(c):
        return copy(part[c].at[1 - core], r1[c], ss1.at[c], rs1.at[c], sibling)

    def c3(c, chip):
        return copy(s3[c].at[chip], r3[c].at[z], ss3.at[c, chip], rs3.at[c, z], device(chip))

    def r3_wait(c, chip):
        copy(s3[c].at[chip], r3[c].at[chip], ss3.at[c, chip], rs3.at[c, chip], device(chip)).wait_recv()

    def encode(c):
        c1(c).wait_recv()
        total = part[c][core] + r1[c][...]
        code = coded(total)
        for k in range(nz):
            own[c][k] = total[k * t:(k + 1) * t, :]
            s3[c][k] = code[k * t:(k + 1) * t, :].astype(jnp.int16)

    def send_same(c):
        for d in range(1, half):
            c3(c, same_tier(d)).start()

    def send_other(c):
        for d in range(half):
            c3(c, other_tier(d)).start()

    @pl.when(tier == 1)
    def _():
        pl.semaphore_wait(barrier, nz)
        for d in range(half):
            greet(late_sem, device(other_tier(d)))

    turn()
    compute(0)

    @pl.when(tier == 0)
    def _():
        pl.semaphore_wait(barrier, half)

    c1(0).start()
    for c in range(chunks):
        if c + 1 < chunks:
            compute(c + 1)
            c1(c + 1).start()
        encode(c)

        @pl.when(tier == 0)
        def _():
            send_same(c)

        @pl.when(tier == 1)
        def _():
            for d in range(half):
                c3(c, d).start()
            send_same(c)

    @pl.when(tier == 0)
    def _():
        pl.semaphore_wait(late_sem, half)
        for c in range(chunks):
            send_other(c)

    for c in range(chunks):
        lo, hi = splits[c]
        total = own[c][z]
        for d in range(1, nz):
            chip = lax.rem(z + d, nz)
            r3_wait(c, chip)
            total = total + decoded(r3[c][chip], (hi - lo) * width)
        for s in range(lo, hi):
            o_ref[s * t:(s + 1) * t, :] = total[:, (s - lo) * width:(s - lo + 1) * width]
    for c in range(chunks):
        c1(c).wait_send()
        for d in range(1, nz):
            c3(c, lax.rem(z + d, nz)).wait_send()


def unfold(t, v_ref, o_ref, lined):
    width = v_ref.shape[1]
    far = width // 2
    value = jnp.concatenate([v_ref[...], jnp.zeros((width * t - v_ref.shape[0], width), jnp.float32)], axis=0)
    lane = lax.broadcasted_iota(jnp.int32, value.shape, 1)
    step = 1
    while step < width:
        value = jnp.where((lane & step) != 0, jnp.roll(value, step * t, axis=0), value)
        step *= 2
    lined[...] = value
    row = lax.broadcasted_iota(jnp.int32, (width, width), 0)
    col = lax.broadcasted_iota(jnp.int32, (width, width), 1)
    near = lax.rem(row - col + width, width) <= far
    for q in range(t):
        at = pl.ds(q, width, stride=t)
        below = lined[at, :]
        lined[at, :] = jnp.where(near, below, below.T)
    per = LANES // width
    for m in range(width // per):
        o_ref[:, m * LANES:(m + 1) * LANES] = jnp.concatenate(
            [lined[(m * per + i) * t:(m * per + i + 1) * t, :] for i in range(per)], axis=1)


def per_device(row_leaves, covariates, query_leaves, leaf_sizes):
    n = lax.axis_size("rows")
    trees, rows = row_leaves.shape
    width = covariates.shape[0]
    queries = query_leaves.shape[1]
    t = queries // n
    nz = n // 2
    sub = nz * t
    cols = [(hi - lo) * width for lo, hi in splits_of(width)]
    chunks = len(cols)
    vmem = pl.BlockSpec(memory_space=pltpu.VMEM)
    f32 = jnp.float32
    i16 = jnp.int16
    dma = pltpu.SemaphoreType.DMA
    folded = pl.pallas_call(
        functools.partial(kernel, n),
        out_shape=pltpu.VMEM(((width // 2 + 1) * t, width), f32),
        in_specs=[pl.BlockSpec(memory_space=pltpu.HBM)] * 4,
        out_specs=vmem,
        scratch_shapes=[
            pltpu.VMEM(row_leaves.shape, jnp.int32),
            pltpu.VMEM(covariates.shape, jnp.bfloat16),
            pltpu.VMEM(query_leaves.shape, jnp.int32),
            pltpu.VMEM(leaf_sizes.shape, jnp.int32),
            pltpu.VMEM((TURNS, width + width // 2, rows), jnp.bfloat16),
            pltpu.VMEM((trees, queries, STEP), i16),
            pltpu.VMEM((trees, queries, STEP), i16),
            pltpu.VMEM((queries, rows), jnp.bfloat16),
            pltpu.VMEM((queries, queries), jnp.bfloat16),
            pltpu.VMEM((trees, trees * LANES), jnp.bfloat16),
            pltpu.SemaphoreType.REGULAR,
            dma((3,)), dma((rows // STEP,)),
            dma((chunks,)), dma((chunks,)),
            dma((chunks, nz)), dma((chunks, nz)),
            *[pltpu.VMEM((2, sub, c), f32) for c in cols],
            *[pltpu.VMEM((nz, t, c), f32) for c in cols],
            *[pltpu.VMEM((nz, t, coded_width(c)), i16) for c in cols],
            *[pltpu.VMEM((sub, c), f32) for c in cols],
            *[pltpu.VMEM((nz, t, coded_width(c)), i16) for c in cols],
        ],
        compiler_params=pltpu.CompilerParams(collective_id=0, has_side_effects=True,
                                             vmem_limit_bytes=56 << 20),
    )(row_leaves, covariates, query_leaves, leaf_sizes)
    return pl.pallas_call(
        functools.partial(unfold, t),
        out_shape=jax.ShapeDtypeStruct((t, width * width), f32),
        in_specs=[vmem],
        out_specs=vmem,
        scratch_shapes=[pltpu.VMEM((width * t, width), f32)],
        compiler_params=pltpu.CompilerParams(vmem_limit_bytes=16 << 20),
    )(folded)


def solution(mesh):
    return jax.shard_map(
        per_device,
        mesh=mesh,
        in_specs=(
            P(None, ("groups", "rows")),
            P(None, ("groups", "rows")),
            P(None, "groups"),
            P("groups", None),
        ),
        out_specs=P(("groups", "rows"), None),
        check_vma=False,
    )
```

```python
import functools

import jax
import jax.numpy as jnp
from jax import lax
from jax.experimental import pallas as pl
from jax.experimental.pallas import tpu as pltpu
from jax.sharding import PartitionSpec as P

LANES = 128
STEP = 256
TURNS = 8
PIECES = 2


def splits_of(width):
    return [(0, width // 4), (width // 4, width // 2 + 1)]


def coded(value):
    largest = jnp.maximum(jnp.max(jnp.abs(value), axis=1, keepdims=True), 1e-30)
    power = jnp.floor(256.0 * jnp.log2(32000.0 / largest))
    whole = jnp.round(value * jnp.exp2(power * (1.0 / 256.0))).astype(jnp.int32)
    spare = -value.shape[1] % LANES or LANES
    tail = jnp.broadcast_to(power.astype(jnp.int32), (value.shape[0], spare))
    return jnp.concatenate([whole, tail], axis=1)


def coded_width(cols):
    return cols + (-cols % LANES or LANES)


def decoded(code, cols):
    wide = code.astype(jnp.int32).astype(jnp.float32)
    return wide[:, :cols] * jnp.exp2(wide[:, cols:cols + 1] * (-1.0 / 256.0))


def kernel(n, rl_hbm, x_hbm, ql_hbm, ls_hbm, o_ref, rl, x, ql, ls, turns, qb, wb, w_s, order, spread, late_sem, in_sems, rl_sems,
           ss1, rs1, ss3, rs3, ss5, rs5, *bufs):
    trees, rows = rl.shape
    width = x.shape[0]
    queries = ql.shape[1]
    splits = splits_of(width)
    chunks = len(splits)
    part, own, s3, r1, r3, s5, r5 = (bufs[i * chunks:(i + 1) * chunks] for i in range(7))
    t = queries // n
    nz = n // 2
    half = nz // 2
    sub = nz * t
    me = lax.axis_index("rows")
    core = lax.rem(me, 2)
    z = me // 2
    tier = z // half
    spot = lax.rem(z, half)
    sibling = me + 1 - 2 * core

    def device(chip):
        return chip * 2 + core

    def same_tier(d):
        return tier * half + lax.rem(spot + d, half)

    def other_tier(d):
        return (1 - tier) * half + lax.rem(spot + d, half)

    def greet(sem, peer):
        pl.semaphore_signal(sem, inc=1, device_id={"rows": peer}, device_id_type=pl.DeviceIdType.MESH)

    def rl_copy(step):
        at = pl.ds(pl.multiple_of(step * STEP, STEP), STEP)
        return pltpu.make_async_copy(rl_hbm.at[:, at], rl.at[:, at], rl_sems.at[step])

    ins = [pltpu.make_async_copy(a, b, in_sems.at[i])
           for i, (a, b) in enumerate(((ls_hbm, ls), (ql_hbm, ql), (x_hbm, x)))]
    ins[0].start()
    ins[1].start()
    for step in range(rows // STEP):
        rl_copy(step).start()
    ins[2].start()

    barrier = pltpu.get_barrier_semaphore()
    greet(barrier, sibling)
    for d in range(1, half):
        greet(barrier, device(same_tier(d)))

    @pl.when(tier == 0)
    def _():
        for d in range(half):
            greet(barrier, device(other_tier(d)))

    @pl.when(z == 0)
    def _():
        for d in range(half):
            greet(barrier, other_tier(d) * 2 + 1 - core)

    bf16 = jnp.bfloat16
    place = lax.broadcasted_iota(jnp.int32, (queries, queries), 0)
    query = lax.broadcasted_iota(jnp.int32, (queries, queries), 1)
    pick = (lax.rem(place, sub) // t * 2 + place // sub) * t + lax.rem(place, t)
    order[...] = jnp.where(query == pick, 1.0, 0.0).astype(bf16)
    tree_of = lax.broadcasted_iota(jnp.int32, (trees, trees * LANES), 1) // LANES
    tree_at = lax.broadcasted_iota(jnp.int32, (trees, trees * LANES), 0)
    spread[...] = jnp.where(tree_of == tree_at, 1.0, 0.0).astype(bf16)
    ins[0].wait()
    ins[1].wait()

    units = float(128 * trees * 2 * rows * n // ls.shape[1])
    inverse = 1.0 / (trees * ls[...].astype(jnp.float32))
    chosen = []
    for first in range(0, queries, LANES):
        piece = ql[:, first:first + LANES]
        wide = piece.shape[1]
        if wide < LANES:
            piece = jnp.concatenate([piece] * (LANES // wide), axis=1)
        chosen.append(jnp.take_along_axis(inverse, piece, axis=1)[:, :wide])
    chosen = jnp.concatenate(chosen, axis=1).astype(bf16) * bf16(units)
    for table, out in ((ql[...].astype(jnp.float32).astype(bf16), qb), (chosen, wb)):
        sorted_t = lax.dot_general(order[...], table, (((1,), (1,)), ((), ())), preferred_element_type=jnp.float32)
        wide = jnp.dot(sorted_t.astype(bf16), spread[...], preferred_element_type=jnp.float32).astype(jnp.int32)
        for b in range(trees):
            one = wide[:, b * LANES:(b + 1) * LANES]
            out[b] = jnp.concatenate([one] * (STEP // LANES), axis=1).astype(jnp.int16)

    tile = 64
    share = 8

    def weights_step(step, carry):
        ats = [pl.ds(pl.multiple_of((step * PIECES + i) * STEP, STEP), STEP) for i in range(PIECES)]
        for i in range(PIECES):
            rl_copy(step * PIECES + i).wait()
        for q0 in range(0, queries, tile):
            def tree(b, accs):
                leaf = qb[b, q0:q0 + tile, :]
                weight = wb[b, q0:q0 + tile, :]
                out = []
                for at, acc in zip(ats, accs):
                    row = jnp.broadcast_to(rl[pl.ds(b, 1), at], (8, STEP)).astype(jnp.int16)
                    row = jnp.concatenate([row] * (tile // 8), axis=0)
                    out.append(acc + jnp.where(leaf == row, weight, jnp.zeros_like(weight)))
                return tuple(out)

            accs = lax.fori_loop(0, trees, tree, (jnp.zeros((tile, STEP), jnp.int16),) * PIECES, unroll=share)
            for at, acc in zip(ats, accs):
                total = acc.astype(jnp.int32).astype(jnp.float32) * (1.0 / units)
                w_s[q0:q0 + tile, at] = total.astype(jnp.bfloat16)
        return carry

    lax.fori_loop(0, rows // (STEP * PIECES), weights_step, 0)
    ins[2].wait()
    def turn():
        for at in range(0, rows, 2 * STEP):
            wide = x[:, at:at + 2 * STEP].astype(jnp.float32)
            for r in range(TURNS):
                turned = (jnp.roll(wide, -r, axis=0) if r else wide).astype(bf16)
                turns[r, :width, at:at + 2 * STEP] = turned
                turns[r, width:, at:at + 2 * STEP] = turned[:turns.shape[1] - width]

    def compute(c):
        lo, hi = splits[c]
        per = STEP // width
        for s in range(lo, hi, per):
            ends = min(hi, s + per)
            prod = jnp.concatenate(
                [x[...] * turns[e % TURNS, e // TURNS * TURNS:e // TURNS * TURNS + width, :] for e in range(s, ends)], axis=0)
            res = lax.dot_general(w_s[...], prod, (((1,), (1,)), ((), ())), preferred_element_type=jnp.float32)
            for a in range(2):
                part[c][a, :, (s - lo) * width:(ends - lo) * width] = res[a * sub:(a + 1) * sub, :]

    def copy(src, dst, ssem, rsem, peer):
        return pltpu.make_async_remote_copy(src_ref=src, dst_ref=dst, send_sem=ssem, recv_sem=rsem,
                                            device_id={"rows": peer}, device_id_type=pl.DeviceIdType.MESH)

    def c1(c):
        return copy(part[c].at[1 - core], r1[c], ss1.at[c], rs1.at[c], sibling)

    def c3(c, chip):
        return copy(s3[c].at[chip], r3[c].at[z], ss3.at[c, chip], rs3.at[c, z], device(chip))

    def r3_wait(c, chip):
        copy(s3[c].at[chip], r3[c].at[chip], ss3.at[c, chip], rs3.at[c, chip], device(chip)).wait_recv()

    def encode(c):
        c1(c).wait_recv()
        total = part[c][core] + r1[c][...]
        code = coded(total)
        for k in range(nz):
            own[c][k] = total[k * t:(k + 1) * t, :]
            s3[c][k] = code[k * t:(k + 1) * t, :].astype(jnp.int16)

    def c5(c, side):
        return copy(s5[c].at[side], r5[c].at[me - nz], ss5.at[c, side], rs5.at[c, me - nz], side)

    def r5_wait(c, k):
        copy(s5[c].at[0], r5[c].at[k], ss5.at[c, 0], rs5.at[c, k], nz + k).wait_recv()

    def direct(c):
        code = coded(jnp.concatenate([part[c][a][:t, :] for a in range(2)], axis=0))
        for a in range(2):
            s5[c][a] = code[a * t:(a + 1) * t, :].astype(jnp.int16)
            c5(c, a).start()

    def send_same(c, first):
        for d in range(first, half):
            @pl.when(d != spot)
            def _():
                c3(c, tier * half + d).start()

    def send_other(c):
        for d in range(half):
            c3(c, other_tier(d)).start()

    @pl.when(tier == 1)
    def _():
        pl.semaphore_wait(barrier, nz + 1)
        for d in range(half):
            greet(late_sem, device(other_tier(d)))

    turn()
    compute(0)

    @pl.when(tier == 0)
    def _():
        pl.semaphore_wait(barrier, half)

    c1(0).start()

    @pl.when(tier == 1)
    def _():
        direct(0)

    for c in range(chunks):
        if c + 1 < chunks:
            compute(c + 1)
            c1(c + 1).start()

            @pl.when(tier == 1)
            def _():
                direct(c + 1)

        encode(c)

        @pl.when(tier == 0)
        def _():
            send_same(c, 0)

        @pl.when(tier == 1)
        def _():
            for d in range(1, half):
                c3(c, d).start()
            send_same(c, 0)

    @pl.when(tier == 0)
    def _():
        pl.semaphore_wait(late_sem, half)
        for c in range(chunks):
            send_other(c)

    def finish(c, peers, cores):
        lo, hi = splits[c]
        cols = (hi - lo) * width
        total = own[c][z]
        for chip in peers:
            r3_wait(c, chip)
            total = total + decoded(r3[c][chip], cols)
        for k in range(cores):
            r5_wait(c, k)
            total = total + decoded(r5[c][k], cols)
        for s in range(lo, hi):
            o_ref[s * t:(s + 1) * t, :] = total[:, (s - lo) * width:(s - lo + 1) * width]

    others = [lax.rem(z + d, nz) for d in range(1, nz)]

    @pl.when(z == 0)
    def _():
        for c in range(chunks):
            finish(c, list(range(1, half)), nz)

    @pl.when(z != 0)
    def _():
        for c in range(chunks):
            finish(c, others, 0)

    for c in range(chunks):
        c1(c).wait_send()

    @pl.when(tier == 0)
    def _():
        for c in range(chunks):
            for chip in others:
                c3(c, chip).wait_send()

    @pl.when(tier == 1)
    def _():
        for c in range(chunks):
            for d in range(1, half):
                c3(c, d).wait_send()
                c3(c, same_tier(d)).wait_send()
            for side in range(2):
                c5(c, side).wait_send()


def unfold(t, v_ref, o_ref, lined):
    width = v_ref.shape[1]
    far = width // 2
    value = jnp.concatenate([v_ref[...], jnp.zeros((width * t - v_ref.shape[0], width), jnp.float32)], axis=0)
    lane = lax.broadcasted_iota(jnp.int32, value.shape, 1)
    step = 1
    while step < width:
        value = jnp.where((lane & step) != 0, jnp.roll(value, step * t, axis=0), value)
        step *= 2
    lined[...] = value
    row = lax.broadcasted_iota(jnp.int32, (width, width), 0)
    col = lax.broadcasted_iota(jnp.int32, (width, width), 1)
    near = lax.rem(row - col + width, width) <= far
    for q in range(t):
        at = pl.ds(q, width, stride=t)
        below = lined[at, :]
        lined[at, :] = jnp.where(near, below, below.T)
    per = LANES // width
    for m in range(width // per):
        o_ref[:, m * LANES:(m + 1) * LANES] = jnp.concatenate(
            [lined[(m * per + i) * t:(m * per + i + 1) * t, :] for i in range(per)], axis=1)


def per_device(row_leaves, covariates, query_leaves, leaf_sizes):
    n = lax.axis_size("rows")
    trees, rows = row_leaves.shape
    width = covariates.shape[0]
    queries = query_leaves.shape[1]
    t = queries // n
    nz = n // 2
    sub = nz * t
    cols = [(hi - lo) * width for lo, hi in splits_of(width)]
    chunks = len(cols)
    vmem = pl.BlockSpec(memory_space=pltpu.VMEM)
    f32 = jnp.float32
    i16 = jnp.int16
    dma = pltpu.SemaphoreType.DMA
    folded = pl.pallas_call(
        functools.partial(kernel, n),
        out_shape=pltpu.VMEM(((width // 2 + 1) * t, width), f32),
        in_specs=[pl.BlockSpec(memory_space=pltpu.HBM)] * 4,
        out_specs=vmem,
        scratch_shapes=[
            pltpu.VMEM(row_leaves.shape, jnp.int32),
            pltpu.VMEM(covariates.shape, jnp.bfloat16),
            pltpu.VMEM(query_leaves.shape, jnp.int32),
            pltpu.VMEM(leaf_sizes.shape, jnp.int32),
            pltpu.VMEM((TURNS, width + width // 2, rows), jnp.bfloat16),
            pltpu.VMEM((trees, queries, STEP), i16),
            pltpu.VMEM((trees, queries, STEP), i16),
            pltpu.VMEM((queries, rows), jnp.bfloat16),
            pltpu.VMEM((queries, queries), jnp.bfloat16),
            pltpu.VMEM((trees, trees * LANES), jnp.bfloat16),
            pltpu.SemaphoreType.REGULAR,
            dma((3,)), dma((rows // STEP,)),
            dma((chunks,)), dma((chunks,)),
            dma((chunks, nz)), dma((chunks, nz)),
            dma((chunks, 2)), dma((chunks, nz)),
            *[pltpu.VMEM((2, sub, c), f32) for c in cols],
            *[pltpu.VMEM((nz, t, c), f32) for c in cols],
            *[pltpu.VMEM((nz, t, coded_width(c)), i16) for c in cols],
            *[pltpu.VMEM((sub, c), f32) for c in cols],
            *[pltpu.VMEM((nz, t, coded_width(c)), i16) for c in cols],
            *[pltpu.VMEM((2, t, coded_width(c)), i16) for c in cols],
            *[pltpu.VMEM((nz, t, coded_width(c)), i16) for c in cols],
        ],
        compiler_params=pltpu.CompilerParams(collective_id=0, has_side_effects=True,
                                             vmem_limit_bytes=56 << 20),
    )(row_leaves, covariates, query_leaves, leaf_sizes)
    return pl.pallas_call(
        functools.partial(unfold, t),
        out_shape=jax.ShapeDtypeStruct((t, width * width), f32),
        in_specs=[vmem],
        out_specs=vmem,
        scratch_shapes=[pltpu.VMEM((width * t, width), f32)],
        compiler_params=pltpu.CompilerParams(vmem_limit_bytes=16 << 20),
    )(folded)


def solution(mesh):
    return jax.shard_map(
        per_device,
        mesh=mesh,
        in_specs=(
            P(None, ("groups", "rows")),
            P(None, ("groups", "rows")),
            P(None, "groups"),
            P("groups", None),
        ),
        out_specs=P(("groups", "rows"), None),
        check_vma=False,
    )
```

```python
import functools

import jax
import jax.numpy as jnp
from jax import lax
from jax.experimental import pallas as pl
from jax.experimental.pallas import tpu as pltpu
from jax.sharding import PartitionSpec as P

LANES = 128
STEP = 256
TURNS = 8
PIECES = 2


def splits_of(width):
    return [(0, width // 4), (width // 4, width // 2 + 1)]


def power_of(value):
    largest = jnp.maximum(jnp.max(jnp.abs(value), axis=1, keepdims=True), 1e-30)
    return jnp.floor(256.0 * jnp.log2(32000.0 / largest))


def coded(value, power):
    whole = jnp.round(value * jnp.exp2(power * (1.0 / 256.0))).astype(jnp.int32)
    spare = -value.shape[1] % LANES or LANES
    tail = jnp.broadcast_to(power.astype(jnp.int32), (value.shape[0], spare))
    return jnp.concatenate([whole, tail], axis=1)


def coded_width(cols):
    return cols + (-cols % LANES or LANES)


def decoded(code, cols):
    wide = code.astype(jnp.int32).astype(jnp.float32)
    return wide[:, :cols] * jnp.exp2(wide[:, cols:cols + 1] * (-1.0 / 256.0))


def over(value, size):
    return value >> (size.bit_length() - 1) if size & (size - 1) == 0 else value // size


def within(value, size):
    return value & (size - 1) if size & (size - 1) == 0 else lax.rem(value, size)


def kernel(n, rl_hbm, x_hbm, ql_hbm, ls_hbm, o_ref, rl, x, ql, ls, turns, qb, wb, w_s, order, spread, powers, late_sem, in_sems, rl_sems,
           ss1, rs1, ss3, rs3, ss5, rs5, *bufs):
    trees, rows = rl.shape
    width = x.shape[0]
    queries = ql.shape[1]
    splits = splits_of(width)
    chunks = len(splits)
    part, own, s3, r1, r3, s5, r5 = (bufs[i * chunks:(i + 1) * chunks] for i in range(7))
    t = queries // n
    nz = n // 2
    half = nz // 2
    sub = nz * t
    me = lax.axis_index("rows")
    core = lax.rem(me, 2)
    z = me // 2
    tier = z // half
    spot = lax.rem(z, half)
    sibling = me + 1 - 2 * core

    def device(chip):
        return chip * 2 + core

    def same_tier(d):
        return tier * half + lax.rem(spot + d, half)

    def other_tier(d):
        return (1 - tier) * half + lax.rem(spot + d, half)

    def greet(sem, peer):
        pl.semaphore_signal(sem, inc=1, device_id={"rows": peer}, device_id_type=pl.DeviceIdType.MESH)

    def rl_copy(step):
        at = pl.ds(pl.multiple_of(step * PIECES * STEP, PIECES * STEP), PIECES * STEP)
        return pltpu.make_async_copy(rl_hbm.at[:, at], rl.at[:, at], rl_sems.at[step])

    ins = [pltpu.make_async_copy(a, b, in_sems.at[i])
           for i, (a, b) in enumerate(((ls_hbm, ls), (ql_hbm, ql), (x_hbm, x)))]
    ins[0].start()
    ins[1].start()
    for step in range(rows // (PIECES * STEP)):
        rl_copy(step).start()
    ins[2].start()

    barrier = pltpu.get_barrier_semaphore()
    greet(barrier, sibling)
    for d in range(1, half):
        greet(barrier, device(same_tier(d)))

    @pl.when(tier == 0)
    def _():
        for d in range(half):
            greet(barrier, device(other_tier(d)))

    @pl.when(z == 0)
    def _():
        for d in range(half):
            greet(barrier, other_tier(d) * 2 + 1 - core)

    bf16 = jnp.bfloat16
    place = lax.broadcasted_iota(jnp.int32, (queries, queries), 0)
    query = lax.broadcasted_iota(jnp.int32, (queries, queries), 1)
    pick = (over(within(place, sub), t) * 2 + over(place, sub)) * t + within(place, t)
    order[...] = jnp.where(query == pick, 1.0, 0.0).astype(bf16)
    tree_of = over(lax.broadcasted_iota(jnp.int32, (trees, trees * LANES), 1), LANES)
    tree_at = lax.broadcasted_iota(jnp.int32, (trees, trees * LANES), 0)
    spread[...] = jnp.where(tree_of == tree_at, 1.0, 0.0).astype(bf16)
    ins[0].wait()
    ins[1].wait()

    units = float(128 * trees * 2 * rows * n // ls.shape[1])
    inverse = 1.0 / (trees * ls[...].astype(jnp.float32))
    chosen = []
    for first in range(0, queries, LANES):
        piece = ql[:, first:first + LANES]
        wide = piece.shape[1]
        if wide < LANES:
            piece = jnp.concatenate([piece] * (LANES // wide), axis=1)
        chosen.append(jnp.take_along_axis(inverse, piece, axis=1)[:, :wide])
    chosen = jnp.concatenate(chosen, axis=1).astype(bf16) * bf16(units)
    both = jnp.concatenate(
        [lax.dot_general(order[...], table, (((1,), (1,)), ((), ())), preferred_element_type=jnp.float32).astype(bf16)
         for table in (ql[...].astype(jnp.float32).astype(bf16), chosen)], axis=0)
    batch = 4
    for first in range(0, trees, batch):
        wide = jnp.dot(both, spread[:, first * LANES:(first + batch) * LANES],
                       preferred_element_type=jnp.float32).astype(jnp.int32)
        for b in range(first, first + batch):
            one = wide[:, (b - first) * LANES:(b - first + 1) * LANES]
            one = jnp.concatenate([one] * (STEP // LANES), axis=1).astype(jnp.int16)
            qb[b] = one[:queries]
            wb[b] = one[queries:]

    tile = 64
    share = 8

    def weights_step(step, carry):
        ats = [pl.ds(pl.multiple_of((step * PIECES + i) * STEP, STEP), STEP) for i in range(PIECES)]
        rl_copy(step).wait()
        for q0 in range(0, queries, tile):
            def tree(b, accs):
                leaf = qb[b, q0:q0 + tile, :]
                weight = wb[b, q0:q0 + tile, :]
                out = []
                for at, acc in zip(ats, accs):
                    row = jnp.broadcast_to(rl[pl.ds(b, 1), at], (8, STEP)).astype(jnp.int16)
                    row = jnp.concatenate([row] * (tile // 8), axis=0)
                    out.append(acc + jnp.where(leaf == row, weight, jnp.zeros_like(weight)))
                return tuple(out)

            accs = lax.fori_loop(0, trees, tree, (jnp.zeros((tile, STEP), jnp.int16),) * PIECES, unroll=share)
            for at, acc in zip(ats, accs):
                total = acc.astype(jnp.int32).astype(jnp.float32) * (1.0 / units)
                w_s[q0:q0 + tile, at] = total.astype(jnp.bfloat16)
        return carry

    lax.fori_loop(0, rows // (STEP * PIECES), weights_step, 0)
    ins[2].wait()
    def turn():
        for at in range(0, rows, 2 * STEP):
            wide = x[:, at:at + 2 * STEP].astype(jnp.float32)
            for r in range(TURNS):
                turned = (jnp.roll(wide, -r, axis=0) if r else wide).astype(bf16)
                turns[r, :width, at:at + 2 * STEP] = turned
                turns[r, width:, at:at + 2 * STEP] = turned[:turns.shape[1] - width]

    def compute(c):
        lo, hi = splits[c]
        per = STEP // width
        for s in range(lo, hi, per):
            ends = min(hi, s + per)
            prod = jnp.concatenate(
                [x[...] * turns[e % TURNS, e // TURNS * TURNS:e // TURNS * TURNS + width, :] for e in range(s, ends)], axis=0)
            res = lax.dot_general(prod, w_s[...], (((1,), (1,)), ((), ())), preferred_element_type=jnp.float32).T
            for a in range(2):
                part[c][a, :, (s - lo) * width:(ends - lo) * width] = res[a * sub:(a + 1) * sub, :]

    def copy(src, dst, ssem, rsem, peer):
        return pltpu.make_async_remote_copy(src_ref=src, dst_ref=dst, send_sem=ssem, recv_sem=rsem,
                                            device_id={"rows": peer}, device_id_type=pl.DeviceIdType.MESH)

    def c1(c):
        return copy(part[c].at[1 - core], r1[c], ss1.at[c], rs1.at[c], sibling)

    def c3(c, chip):
        return copy(s3[c].at[chip], r3[c].at[z], ss3.at[c, chip], rs3.at[c, z], device(chip))

    def r3_wait(c, chip):
        copy(s3[c].at[chip], r3[c].at[chip], ss3.at[c, chip], rs3.at[c, chip], device(chip)).wait_recv()

    def encode(c):
        c1(c).wait_recv()
        total = part[c][core] + r1[c][...]
        if c == 0:
            powers[:sub] = jnp.broadcast_to(power_of(total), (sub, LANES))
        code = coded(total, powers[:sub, :1])
        for k in range(nz):
            own[c][k] = total[k * t:(k + 1) * t, :]
            s3[c][k] = code[k * t:(k + 1) * t, :].astype(jnp.int16)

    def c5(c, side):
        return copy(s5[c].at[side], r5[c].at[me - nz], ss5.at[c, side], rs5.at[c, me - nz], side)

    def r5_wait(c, k):
        copy(s5[c].at[0], r5[c].at[k], ss5.at[c, 0], rs5.at[c, k], nz + k).wait_recv()

    def direct(c):
        value = jnp.concatenate([part[c][a][:t, :] for a in range(2)], axis=0)
        if c == 0:
            powers[sub:] = jnp.broadcast_to(power_of(value), (2 * t, LANES))
        code = coded(value, powers[sub:, :1])
        for a in range(2):
            s5[c][a] = code[a * t:(a + 1) * t, :].astype(jnp.int16)
            c5(c, a).start()

    def send_same(c, first):
        for d in range(first, half):
            @pl.when(d != spot)
            def _():
                c3(c, tier * half + d).start()

    def send_other(c):
        for d in range(half):
            c3(c, other_tier(d)).start()

    @pl.when(tier == 1)
    def _():
        pl.semaphore_wait(barrier, nz + 1)
        for d in range(half):
            greet(late_sem, device(other_tier(d)))

    turn()
    compute(0)

    @pl.when(tier == 0)
    def _():
        pl.semaphore_wait(barrier, half)


    @pl.when(tier == 1)
    def _():
        direct(0)

    c1(0).start()
    for c in range(chunks):
        if c + 1 < chunks:
            compute(c + 1)

            @pl.when(tier == 1)
            def _():
                direct(c + 1)

            c1(c + 1).start()
        encode(c)

        @pl.when(tier == 0)
        def _():
            send_same(c, 0)

        @pl.when(tier == 1)
        def _():
            for d in range(1, half):
                c3(c, d).start()
            send_same(c, 0)

    @pl.when(tier == 0)
    def _():
        pl.semaphore_wait(late_sem, half)
        for c in range(chunks):
            send_other(c)

    def finish(c, peers, cores):
        lo, hi = splits[c]
        cols = (hi - lo) * width
        total = own[c][z]
        for chip in peers:
            r3_wait(c, chip)
            total = total + decoded(r3[c][chip], cols)
        for k in range(cores):
            r5_wait(c, k)
            total = total + decoded(r5[c][k], cols)
        for s in range(lo, hi):
            o_ref[s * t:(s + 1) * t, :] = total[:, (s - lo) * width:(s - lo + 1) * width]

    others = [lax.rem(z + d, nz) for d in range(1, nz)]

    @pl.when(z == 0)
    def _():
        for c in range(chunks):
            finish(c, list(range(1, half)), nz)

    @pl.when(z != 0)
    def _():
        for c in range(chunks):
            finish(c, others, 0)

    for c in range(chunks):
        c1(c).wait_send()

    @pl.when(tier == 0)
    def _():
        for c in range(chunks):
            for chip in others:
                c3(c, chip).wait_send()

    @pl.when(tier == 1)
    def _():
        for c in range(chunks):
            for d in range(1, half):
                c3(c, d).wait_send()
                c3(c, same_tier(d)).wait_send()
            for side in range(2):
                c5(c, side).wait_send()


def unfold(t, v_ref, o_ref, lined):
    width = v_ref.shape[1]
    far = width // 2
    value = jnp.concatenate([v_ref[...], jnp.zeros((width * t - v_ref.shape[0], width), jnp.float32)], axis=0)
    lane = lax.broadcasted_iota(jnp.int32, value.shape, 1)
    step = 1
    while step < width:
        value = jnp.where((lane & step) != 0, jnp.roll(value, step * t, axis=0), value)
        step *= 2
    lined[...] = value
    row = lax.broadcasted_iota(jnp.int32, (width, width), 0)
    col = lax.broadcasted_iota(jnp.int32, (width, width), 1)
    near = within(row - col + width, width) <= far
    for q in range(t):
        at = pl.ds(q, width, stride=t)
        below = lined[at, :]
        lined[at, :] = jnp.where(near, below, below.T)
    per = LANES // width
    for m in range(width // per):
        o_ref[:, m * LANES:(m + 1) * LANES] = jnp.concatenate(
            [lined[(m * per + i) * t:(m * per + i + 1) * t, :] for i in range(per)], axis=1)


def per_device(row_leaves, covariates, query_leaves, leaf_sizes):
    n = lax.axis_size("rows")
    trees, rows = row_leaves.shape
    width = covariates.shape[0]
    queries = query_leaves.shape[1]
    t = queries // n
    nz = n // 2
    sub = nz * t
    cols = [(hi - lo) * width for lo, hi in splits_of(width)]
    chunks = len(cols)
    vmem = pl.BlockSpec(memory_space=pltpu.VMEM)
    f32 = jnp.float32
    i16 = jnp.int16
    dma = pltpu.SemaphoreType.DMA
    folded = pl.pallas_call(
        functools.partial(kernel, n),
        out_shape=pltpu.VMEM(((width // 2 + 1) * t, width), f32),
        in_specs=[pl.BlockSpec(memory_space=pltpu.HBM)] * 4,
        out_specs=vmem,
        scratch_shapes=[
            pltpu.VMEM(row_leaves.shape, jnp.int32),
            pltpu.VMEM(covariates.shape, jnp.bfloat16),
            pltpu.VMEM(query_leaves.shape, jnp.int32),
            pltpu.VMEM(leaf_sizes.shape, jnp.int32),
            pltpu.VMEM((TURNS, width + width // 2, rows), jnp.bfloat16),
            pltpu.VMEM((trees, queries, STEP), i16),
            pltpu.VMEM((trees, queries, STEP), i16),
            pltpu.VMEM((queries, rows), jnp.bfloat16),
            pltpu.VMEM((queries, queries), jnp.bfloat16),
            pltpu.VMEM((trees, trees * LANES), jnp.bfloat16),
            pltpu.VMEM((sub + 2 * t, LANES), f32),
            pltpu.SemaphoreType.REGULAR,
            dma((3,)), dma((rows // (PIECES * STEP),)),
            dma((chunks,)), dma((chunks,)),
            dma((chunks, nz)), dma((chunks, nz)),
            dma((chunks, 2)), dma((chunks, nz)),
            *[pltpu.VMEM((2, sub, c), f32) for c in cols],
            *[pltpu.VMEM((nz, t, c), f32) for c in cols],
            *[pltpu.VMEM((nz, t, coded_width(c)), i16) for c in cols],
            *[pltpu.VMEM((sub, c), f32) for c in cols],
            *[pltpu.VMEM((nz, t, coded_width(c)), i16) for c in cols],
            *[pltpu.VMEM((2, t, coded_width(c)), i16) for c in cols],
            *[pltpu.VMEM((nz, t, coded_width(c)), i16) for c in cols],
        ],
        compiler_params=pltpu.CompilerParams(collective_id=0, has_side_effects=True,
                                             vmem_limit_bytes=56 << 20),
    )(row_leaves, covariates, query_leaves, leaf_sizes)
    return pl.pallas_call(
        functools.partial(unfold, t),
        out_shape=jax.ShapeDtypeStruct((t, width * width), f32),
        in_specs=[vmem],
        out_specs=vmem,
        scratch_shapes=[pltpu.VMEM((width * t, width), f32)],
        compiler_params=pltpu.CompilerParams(vmem_limit_bytes=16 << 20),
    )(folded)


def solution(mesh):
    return jax.shard_map(
        per_device,
        mesh=mesh,
        in_specs=(
            P(None, ("groups", "rows")),
            P(None, ("groups", "rows")),
            P(None, "groups"),
            P("groups", None),
        ),
        out_specs=P(("groups", "rows"), None),
        check_vma=False,
    )
```

```python
import functools

import jax
import jax.numpy as jnp
from jax import lax
from jax.experimental import pallas as pl
from jax.experimental.pallas import tpu as pltpu
from jax.sharding import PartitionSpec as P

LANES = 128
STEP = 256
TURNS = 8
PIECES = 2


def splits_of(width):
    return [(0, width // 4), (width // 4, width // 2 + 1)]


def power_of(value):
    largest = jnp.maximum(jnp.max(jnp.abs(value), axis=1, keepdims=True), 1e-30)
    return jnp.floor(256.0 * jnp.log2(32000.0 / largest))


def coded(value, power):
    whole = jnp.round(value * jnp.exp2(power * (1.0 / 256.0))).astype(jnp.int32)
    spare = -value.shape[1] % LANES or LANES
    tail = jnp.broadcast_to(power.astype(jnp.int32), (value.shape[0], spare))
    return jnp.concatenate([whole, tail], axis=1)


def coded_width(cols):
    return cols + (-cols % LANES or LANES)


def over(value, size):
    return value >> (size.bit_length() - 1) if size & (size - 1) == 0 else value // size


def within(value, size):
    return value & (size - 1) if size & (size - 1) == 0 else lax.rem(value, size)


def kernel(n, rl_hbm, x_hbm, ql_hbm, ls_hbm, o_ref, rl, x, ql, ls, turns, qb, wb, w_s, order, spread, powers, late_sem, in_sems, rl_sems,
           ss1, rs1, ss3, rs3, ss5, rs5, *bufs):
    trees, rows = rl.shape
    width = x.shape[0]
    queries = ql.shape[1]
    splits = splits_of(width)
    chunks = len(splits)
    part, own, s3, r1, r3, s5, r5 = (bufs[i * chunks:(i + 1) * chunks] for i in range(7))
    t = queries // n
    nz = n // 2
    half = nz // 2
    sub = nz * t
    me = lax.axis_index("rows")
    core = lax.rem(me, 2)
    z = me // 2
    tier = z // half
    spot = lax.rem(z, half)
    sibling = me + 1 - 2 * core

    def device(chip):
        return chip * 2 + core

    def same_tier(d):
        return tier * half + lax.rem(spot + d, half)

    def other_tier(d):
        return (1 - tier) * half + lax.rem(spot + d, half)

    def greet(sem, peer):
        pl.semaphore_signal(sem, inc=1, device_id={"rows": peer}, device_id_type=pl.DeviceIdType.MESH)

    def rl_copy(step):
        at = pl.ds(pl.multiple_of(step * PIECES * STEP, PIECES * STEP), PIECES * STEP)
        return pltpu.make_async_copy(rl_hbm.at[:, at], rl.at[:, at], rl_sems.at[step])

    ins = [pltpu.make_async_copy(a, b, in_sems.at[i])
           for i, (a, b) in enumerate(((ls_hbm, ls), (ql_hbm, ql), (x_hbm, x)))]
    ins[0].start()
    ins[1].start()
    for step in range(rows // (PIECES * STEP)):
        rl_copy(step).start()
    ins[2].start()

    barrier = pltpu.get_barrier_semaphore()
    greet(barrier, sibling)
    for d in range(1, half):
        greet(barrier, device(same_tier(d)))

    @pl.when(tier == 0)
    def _():
        for d in range(half):
            greet(barrier, device(other_tier(d)))

    @pl.when(z == 0)
    def _():
        for d in range(half):
            greet(barrier, other_tier(d) * 2 + 1 - core)

    bf16 = jnp.bfloat16
    place = lax.broadcasted_iota(jnp.int32, (queries, queries), 0)
    query = lax.broadcasted_iota(jnp.int32, (queries, queries), 1)
    pick = (over(within(place, sub), t) * 2 + over(place, sub)) * t + within(place, t)
    order[...] = jnp.where(query == pick, 1.0, 0.0).astype(bf16)
    tree_of = over(lax.broadcasted_iota(jnp.int32, (trees, trees * LANES), 1), LANES)
    tree_at = lax.broadcasted_iota(jnp.int32, (trees, trees * LANES), 0)
    spread[...] = jnp.where(tree_of == tree_at, 1.0, 0.0).astype(bf16)
    ins[0].wait()
    ins[1].wait()

    units = float(128 * trees * 2 * rows * n // ls.shape[1])
    inverse = 1.0 / (trees * ls[...].astype(jnp.float32))
    chosen = []
    for first in range(0, queries, LANES):
        piece = ql[:, first:first + LANES]
        wide = piece.shape[1]
        if wide < LANES:
            piece = jnp.concatenate([piece] * (LANES // wide), axis=1)
        chosen.append(jnp.take_along_axis(inverse, piece, axis=1)[:, :wide])
    chosen = jnp.concatenate(chosen, axis=1).astype(bf16) * bf16(units)
    both = jnp.concatenate(
        [lax.dot_general(order[...], table, (((1,), (1,)), ((), ())), preferred_element_type=jnp.float32).astype(bf16)
         for table in (ql[...].astype(jnp.float32).astype(bf16), chosen)], axis=0)
    batch = 4
    for first in range(0, trees, batch):
        wide = jnp.dot(both, spread[:, first * LANES:(first + batch) * LANES],
                       preferred_element_type=jnp.float32).astype(jnp.int32)
        for b in range(first, first + batch):
            one = wide[:, (b - first) * LANES:(b - first + 1) * LANES]
            one = jnp.concatenate([one] * (STEP // LANES), axis=1).astype(jnp.int16)
            qb[b] = one[:queries]
            wb[b] = one[queries:]

    tile = 64
    share = 8

    def weights_step(step, carry):
        ats = [pl.ds(pl.multiple_of((step * PIECES + i) * STEP, STEP), STEP) for i in range(PIECES)]
        rl_copy(step).wait()
        for q0 in range(0, queries, tile):
            def tree(b, accs):
                leaf = qb[b, q0:q0 + tile, :]
                weight = wb[b, q0:q0 + tile, :]
                out = []
                for at, acc in zip(ats, accs):
                    row = jnp.broadcast_to(rl[pl.ds(b, 1), at], (8, STEP)).astype(jnp.int16)
                    row = jnp.concatenate([row] * (tile // 8), axis=0)
                    out.append(acc + jnp.where(leaf == row, weight, jnp.zeros_like(weight)))
                return tuple(out)

            accs = lax.fori_loop(0, trees, tree, (jnp.zeros((tile, STEP), jnp.int16),) * PIECES, unroll=share)
            for at, acc in zip(ats, accs):
                total = acc.astype(jnp.int32).astype(jnp.float32) * (1.0 / units)
                w_s[q0:q0 + tile, at] = total.astype(jnp.bfloat16)
        return carry

    lax.fori_loop(0, rows // (STEP * PIECES), weights_step, 0)
    ins[2].wait()
    def turn():
        for at in range(0, rows, 2 * STEP):
            wide = x[:, at:at + 2 * STEP].astype(jnp.float32)
            for r in range(TURNS):
                turned = (jnp.roll(wide, -r, axis=0) if r else wide).astype(bf16)
                turns[r, :width, at:at + 2 * STEP] = turned
                turns[r, width:, at:at + 2 * STEP] = turned[:turns.shape[1] - width]

    def compute(c):
        lo, hi = splits[c]
        per = STEP // width
        for s in range(lo, hi, per):
            ends = min(hi, s + per)
            prod = jnp.concatenate(
                [x[...] * turns[e % TURNS, e // TURNS * TURNS:e // TURNS * TURNS + width, :] for e in range(s, ends)], axis=0)
            res = lax.dot_general(prod, w_s[...], (((1,), (1,)), ((), ())), preferred_element_type=jnp.float32).T
            for a in range(2):
                part[c][a, :, (s - lo) * width:(ends - lo) * width] = res[a * sub:(a + 1) * sub, :]

    def copy(src, dst, ssem, rsem, peer):
        return pltpu.make_async_remote_copy(src_ref=src, dst_ref=dst, send_sem=ssem, recv_sem=rsem,
                                            device_id={"rows": peer}, device_id_type=pl.DeviceIdType.MESH)

    def c1(c):
        return copy(part[c].at[1 - core], r1[c], ss1.at[c], rs1.at[c], sibling)

    def c3(c, chip):
        return copy(s3[c].at[chip], r3[c].at[z], ss3.at[c, chip], rs3.at[c, z], device(chip))

    def r3_wait(c, chip):
        copy(s3[c].at[chip], r3[c].at[chip], ss3.at[c, chip], rs3.at[c, chip], device(chip)).wait_recv()

    def encode(c):
        c1(c).wait_recv()
        total = part[c][core] + r1[c][...]
        if c == 0:
            powers[:sub] = jnp.broadcast_to(power_of(total), (sub, LANES))
        code = coded(total, powers[:sub, :1])
        for k in range(nz):
            own[c][k] = total[k * t:(k + 1) * t, :]
            s3[c][k] = code[k * t:(k + 1) * t, :].astype(jnp.int16)

    def c5(c, side):
        return copy(s5[c].at[side], r5[c].at[me - nz], ss5.at[c, side], rs5.at[c, me - nz], side)

    def r5_wait(c, k):
        copy(s5[c].at[0], r5[c].at[k], ss5.at[c, 0], rs5.at[c, k], nz + k).wait_recv()

    def direct(c):
        value = jnp.concatenate([part[c][a][:t, :] for a in range(2)], axis=0)
        if c == 0:
            powers[sub:] = jnp.broadcast_to(power_of(value), (2 * t, LANES))
        code = coded(value, powers[sub:, :1])
        for a in range(2):
            s5[c][a] = code[a * t:(a + 1) * t, :].astype(jnp.int16)
            c5(c, a).start()

    def send_same(c, first):
        for d in range(first, half):
            @pl.when(d != spot)
            def _():
                c3(c, tier * half + d).start()

    def send_other(c):
        for d in range(half):
            c3(c, other_tier(d)).start()

    @pl.when(tier == 1)
    def _():
        pl.semaphore_wait(barrier, nz + 1)
        for d in range(half):
            greet(late_sem, device(other_tier(d)))

    turn()
    compute(0)

    @pl.when(tier == 0)
    def _():
        pl.semaphore_wait(barrier, half)


    @pl.when(tier == 1)
    def _():
        direct(0)

    c1(0).start()
    for c in range(chunks):
        if c + 1 < chunks:
            compute(c + 1)

            @pl.when(tier == 1)
            def _():
                direct(c + 1)

            c1(c + 1).start()
        encode(c)

        @pl.when(tier == 0)
        def _():
            send_same(c, 0)

        @pl.when(tier == 1)
        def _():
            for d in range(1, half):
                c3(c, d).start()
            send_same(c, 0)

    @pl.when(tier == 0)
    def _():
        pl.semaphore_wait(late_sem, half)
        for c in range(chunks):
            send_other(c)

    others = [lax.rem(z + d, nz) for d in range(1, nz)]

    def number(code):
        return code.astype(jnp.int32).astype(jnp.float32)

    def finish(chips, cores):
        sources = [(r3, chip) for chip in chips] + [(r5, k) for k in range(cores)]
        scales = []
        for c in range(chunks):
            lo, hi = splits[c]
            cols = (hi - lo) * width
            for chip in chips:
                r3_wait(c, chip)
            for k in range(cores):
                r5_wait(c, k)
            if c == 0:
                scales = [jnp.exp2(number(r[c][at, :, cols:cols + LANES]) * (-1.0 / 256.0)) for r, at in sources]
            for at in range(0, cols, LANES):
                end = min(at + LANES, cols)
                total = own[c][z, :, at:end]
                for (r, src), scale in zip(sources, scales):
                    total = total + number(r[c][src, :, at:end]) * scale[:, :end - at]
                for s in range(lo + at // width, lo + end // width):
                    o_ref[s * t:(s + 1) * t, :] = total[:, (s - lo) * width - at:(s - lo + 1) * width - at]

    @pl.when(z == 0)
    def _():
        finish(list(range(1, half)), nz)

    @pl.when(z != 0)
    def _():
        finish(others, 0)

    for c in range(chunks):
        c1(c).wait_send()

    @pl.when(tier == 0)
    def _():
        for c in range(chunks):
            for chip in others:
                c3(c, chip).wait_send()

    @pl.when(tier == 1)
    def _():
        for c in range(chunks):
            for d in range(1, half):
                c3(c, d).wait_send()
                c3(c, same_tier(d)).wait_send()
            for side in range(2):
                c5(c, side).wait_send()


def unfold(t, v_ref, o_ref, lined):
    width = v_ref.shape[1]
    far = width // 2
    value = jnp.concatenate([v_ref[...], jnp.zeros((width * t - v_ref.shape[0], width), jnp.float32)], axis=0)
    lane = lax.broadcasted_iota(jnp.int32, value.shape, 1)
    step = 1
    while step < width:
        value = jnp.where((lane & step) != 0, jnp.roll(value, step * t, axis=0), value)
        step *= 2
    lined[...] = value
    row = lax.broadcasted_iota(jnp.int32, (width, width), 0)
    col = lax.broadcasted_iota(jnp.int32, (width, width), 1)
    near = within(row - col + width, width) <= far
    for q in range(t):
        at = pl.ds(q, width, stride=t)
        below = lined[at, :]
        lined[at, :] = jnp.where(near, below, below.T)
    per = LANES // width
    for m in range(width // per):
        o_ref[:, m * LANES:(m + 1) * LANES] = jnp.concatenate(
            [lined[(m * per + i) * t:(m * per + i + 1) * t, :] for i in range(per)], axis=1)


def per_device(row_leaves, covariates, query_leaves, leaf_sizes):
    n = lax.axis_size("rows")
    trees, rows = row_leaves.shape
    width = covariates.shape[0]
    queries = query_leaves.shape[1]
    t = queries // n
    nz = n // 2
    sub = nz * t
    cols = [(hi - lo) * width for lo, hi in splits_of(width)]
    chunks = len(cols)
    vmem = pl.BlockSpec(memory_space=pltpu.VMEM)
    f32 = jnp.float32
    i16 = jnp.int16
    dma = pltpu.SemaphoreType.DMA
    folded = pl.pallas_call(
        functools.partial(kernel, n),
        out_shape=pltpu.VMEM(((width // 2 + 1) * t, width), f32),
        in_specs=[pl.BlockSpec(memory_space=pltpu.HBM)] * 4,
        out_specs=vmem,
        scratch_shapes=[
            pltpu.VMEM(row_leaves.shape, jnp.int32),
            pltpu.VMEM(covariates.shape, jnp.bfloat16),
            pltpu.VMEM(query_leaves.shape, jnp.int32),
            pltpu.VMEM(leaf_sizes.shape, jnp.int32),
            pltpu.VMEM((TURNS, width + width // 2, rows), jnp.bfloat16),
            pltpu.VMEM((trees, queries, STEP), i16),
            pltpu.VMEM((trees, queries, STEP), i16),
            pltpu.VMEM((queries, rows), jnp.bfloat16),
            pltpu.VMEM((queries, queries), jnp.bfloat16),
            pltpu.VMEM((trees, trees * LANES), jnp.bfloat16),
            pltpu.VMEM((sub + 2 * t, LANES), f32),
            pltpu.SemaphoreType.REGULAR,
            dma((3,)), dma((rows // (PIECES * STEP),)),
            dma((chunks,)), dma((chunks,)),
            dma((chunks, nz)), dma((chunks, nz)),
            dma((chunks, 2)), dma((chunks, nz)),
            *[pltpu.VMEM((2, sub, c), f32) for c in cols],
            *[pltpu.VMEM((nz, t, c), f32) for c in cols],
            *[pltpu.VMEM((nz, t, coded_width(c)), i16) for c in cols],
            *[pltpu.VMEM((sub, c), f32) for c in cols],
            *[pltpu.VMEM((nz, t, coded_width(c)), i16) for c in cols],
            *[pltpu.VMEM((2, t, coded_width(c)), i16) for c in cols],
            *[pltpu.VMEM((nz, t, coded_width(c)), i16) for c in cols],
        ],
        compiler_params=pltpu.CompilerParams(collective_id=0, has_side_effects=True,
                                             vmem_limit_bytes=56 << 20),
    )(row_leaves, covariates, query_leaves, leaf_sizes)
    return pl.pallas_call(
        functools.partial(unfold, t),
        out_shape=jax.ShapeDtypeStruct((t, width * width), f32),
        in_specs=[vmem],
        out_specs=vmem,
        scratch_shapes=[pltpu.VMEM((width * t, width), f32)],
        compiler_params=pltpu.CompilerParams(vmem_limit_bytes=16 << 20),
    )(folded)


def solution(mesh):
    return jax.shard_map(
        per_device,
        mesh=mesh,
        in_specs=(
            P(None, ("groups", "rows")),
            P(None, ("groups", "rows")),
            P(None, "groups"),
            P("groups", None),
        ),
        out_specs=P(("groups", "rows"), None),
        check_vma=False,
    )
```

```python
import functools

import jax
import jax.numpy as jnp
from jax import lax
from jax.experimental import pallas as pl
from jax.experimental.pallas import tpu as pltpu
from jax.sharding import PartitionSpec as P

LANES = 128
STEP = 256
TURNS = 8
PIECES = 2


def splits_of(width):
    return [(0, width // 4), (width // 4, width // 2 + 1)]


def power_of(value):
    largest = jnp.maximum(jnp.max(jnp.abs(value), axis=1, keepdims=True), 1e-30)
    return jnp.floor(256.0 * jnp.log2(32000.0 / jnp.broadcast_to(largest, (value.shape[0], LANES))))


def coded(value, power):
    scale = jnp.exp2(power * (1.0 / 256.0))
    pieces = []
    for at in range(0, value.shape[1], LANES):
        piece = value[:, at:at + LANES]
        pieces.append(jnp.round(piece * scale[:, :piece.shape[1]]).astype(jnp.int32))
    spare = -value.shape[1] % LANES or LANES
    return jnp.concatenate(pieces + [power[:, :spare].astype(jnp.int32)], axis=1)


def coded_width(cols):
    return cols + (-cols % LANES or LANES)


def over(value, size):
    return value >> (size.bit_length() - 1) if size & (size - 1) == 0 else value // size


def within(value, size):
    return value & (size - 1) if size & (size - 1) == 0 else lax.rem(value, size)


def kernel(n, rl_hbm, x_hbm, ql_hbm, ls_hbm, o_ref, rl, x, ql, ls, turns, qb, wb, w_s, order, spread, powers, late_sem, in_sems, rl_sems,
           ss1, rs1, ss3, rs3, ss5, rs5, *bufs):
    trees, rows = rl.shape
    width = x.shape[0]
    queries = ql.shape[1]
    splits = splits_of(width)
    chunks = len(splits)
    part, own, s3, r1, r3, s5, r5 = (bufs[i * chunks:(i + 1) * chunks] for i in range(7))
    t = queries // n
    nz = n // 2
    half = nz // 2
    sub = nz * t
    me = lax.axis_index("rows")
    core = lax.rem(me, 2)
    z = me // 2
    tier = z // half
    spot = lax.rem(z, half)
    sibling = me + 1 - 2 * core

    def device(chip):
        return chip * 2 + core

    def same_tier(d):
        return tier * half + lax.rem(spot + d, half)

    def other_tier(d):
        return (1 - tier) * half + lax.rem(spot + d, half)

    def greet(sem, peer):
        pl.semaphore_signal(sem, inc=1, device_id={"rows": peer}, device_id_type=pl.DeviceIdType.MESH)

    def rl_copy(step):
        at = pl.ds(pl.multiple_of(step * PIECES * STEP, PIECES * STEP), PIECES * STEP)
        return pltpu.make_async_copy(rl_hbm.at[:, at], rl.at[:, at], rl_sems.at[step])

    ins = [pltpu.make_async_copy(a, b, in_sems.at[i])
           for i, (a, b) in enumerate(((ls_hbm, ls), (ql_hbm, ql), (x_hbm, x)))]
    ins[0].start()
    ins[1].start()
    for step in range(rows // (PIECES * STEP)):
        rl_copy(step).start()
    ins[2].start()

    barrier = pltpu.get_barrier_semaphore()
    greet(barrier, sibling)
    for d in range(1, half):
        greet(barrier, device(same_tier(d)))

    @pl.when(tier == 0)
    def _():
        for d in range(half):
            greet(barrier, device(other_tier(d)))

    @pl.when(z == 0)
    def _():
        for d in range(half):
            greet(barrier, other_tier(d) * 2 + 1 - core)

    bf16 = jnp.bfloat16
    place = lax.broadcasted_iota(jnp.int32, (queries, queries), 0)
    query = lax.broadcasted_iota(jnp.int32, (queries, queries), 1)
    pick = (over(within(place, sub), t) * 2 + over(place, sub)) * t + within(place, t)
    order[...] = jnp.where(query == pick, 1.0, 0.0).astype(bf16)
    tree_of = over(lax.broadcasted_iota(jnp.int32, (trees, trees * LANES), 1), LANES)
    tree_at = lax.broadcasted_iota(jnp.int32, (trees, trees * LANES), 0)
    spread[...] = jnp.where(tree_of == tree_at, 1.0, 0.0).astype(bf16)
    ins[0].wait()
    ins[1].wait()

    units = float(128 * trees * 2 * rows * n // ls.shape[1])
    inverse = 1.0 / (trees * ls[...].astype(jnp.float32))
    chosen = []
    for first in range(0, queries, LANES):
        piece = ql[:, first:first + LANES]
        wide = piece.shape[1]
        if wide < LANES:
            piece = jnp.concatenate([piece] * (LANES // wide), axis=1)
        chosen.append(jnp.take_along_axis(inverse, piece, axis=1)[:, :wide])
    chosen = jnp.concatenate(chosen, axis=1).astype(bf16) * bf16(units)
    both = jnp.concatenate(
        [lax.dot_general(order[...], table, (((1,), (1,)), ((), ())), preferred_element_type=jnp.float32).astype(bf16)
         for table in (ql[...].astype(jnp.float32).astype(bf16), chosen)], axis=0)
    batch = 4
    for first in range(0, trees, batch):
        wide = jnp.dot(both, spread[:, first * LANES:(first + batch) * LANES],
                       preferred_element_type=jnp.float32).astype(jnp.int32)
        for b in range(first, first + batch):
            one = wide[:, (b - first) * LANES:(b - first + 1) * LANES]
            one = jnp.concatenate([one] * (STEP // LANES), axis=1).astype(jnp.int16)
            qb[b] = one[:queries]
            wb[b] = one[queries:]

    tile = 64
    share = 8

    def weights_step(step, carry):
        ats = [pl.ds(pl.multiple_of((step * PIECES + i) * STEP, STEP), STEP) for i in range(PIECES)]
        rl_copy(step).wait()
        for q0 in range(0, queries, tile):
            def tree(b, accs):
                leaf = qb[b, q0:q0 + tile, :]
                weight = wb[b, q0:q0 + tile, :]
                out = []
                for at, acc in zip(ats, accs):
                    row = jnp.broadcast_to(rl[pl.ds(b, 1), at], (8, STEP)).astype(jnp.int16)
                    row = jnp.concatenate([row] * (tile // 8), axis=0)
                    out.append(acc + jnp.where(leaf == row, weight, jnp.zeros_like(weight)))
                return tuple(out)

            accs = lax.fori_loop(0, trees, tree, (jnp.zeros((tile, STEP), jnp.int16),) * PIECES, unroll=share)
            for at, acc in zip(ats, accs):
                total = acc.astype(jnp.int32).astype(jnp.float32) * (1.0 / units)
                w_s[q0:q0 + tile, at] = total.astype(jnp.bfloat16)
        return carry

    lax.fori_loop(0, rows // (STEP * PIECES), weights_step, 0)
    ins[2].wait()
    def turn():
        for at in range(0, rows, 2 * STEP):
            wide = x[:, at:at + 2 * STEP].astype(jnp.float32)
            for r in range(TURNS):
                turned = (jnp.roll(wide, -r, axis=0) if r else wide).astype(bf16)
                turns[r, :width, at:at + 2 * STEP] = turned
                turns[r, width:, at:at + 2 * STEP] = turned[:turns.shape[1] - width]

    def compute(c):
        lo, hi = splits[c]
        per = STEP // width
        for s in range(lo, hi, per):
            ends = min(hi, s + per)
            prod = jnp.concatenate(
                [x[...] * turns[e % TURNS, e // TURNS * TURNS:e // TURNS * TURNS + width, :] for e in range(s, ends)], axis=0)
            res = lax.dot_general(prod, w_s[...], (((1,), (1,)), ((), ())), preferred_element_type=jnp.float32).T
            for a in range(2):
                part[c][a, :, (s - lo) * width:(ends - lo) * width] = res[a * sub:(a + 1) * sub, :]

    def copy(src, dst, ssem, rsem, peer):
        return pltpu.make_async_remote_copy(src_ref=src, dst_ref=dst, send_sem=ssem, recv_sem=rsem,
                                            device_id={"rows": peer}, device_id_type=pl.DeviceIdType.MESH)

    def c1(c):
        return copy(part[c].at[1 - core], r1[c], ss1.at[c], rs1.at[c], sibling)

    def c3(c, chip):
        return copy(s3[c].at[chip], r3[c].at[z], ss3.at[c, chip], rs3.at[c, z], device(chip))

    def r3_wait(c, chip):
        copy(s3[c].at[chip], r3[c].at[chip], ss3.at[c, chip], rs3.at[c, chip], device(chip)).wait_recv()

    def encode(c):
        c1(c).wait_recv()
        total = part[c][core] + r1[c][...]
        if c == 0:
            power = power_of(total[:, :width])
            powers[:sub] = power
        else:
            power = powers[:sub]
        code = coded(total, power)
        for k in range(nz):
            own[c][k] = total[k * t:(k + 1) * t, :]
            s3[c][k] = code[k * t:(k + 1) * t, :].astype(jnp.int16)

    def c5(c, side):
        return copy(s5[c].at[side], r5[c].at[me - nz], ss5.at[c, side], rs5.at[c, me - nz], side)

    def r5_wait(c, k):
        copy(s5[c].at[0], r5[c].at[k], ss5.at[c, 0], rs5.at[c, k], nz + k).wait_recv()

    def direct(c):
        value = jnp.concatenate([part[c][a][:t, :] for a in range(2)], axis=0)
        if c == 0:
            power = power_of(value[:, :width])
            powers[sub:] = power
        else:
            power = powers[sub:]
        code = coded(value, power)
        for a in range(2):
            s5[c][a] = code[a * t:(a + 1) * t, :].astype(jnp.int16)
            c5(c, a).start()

    def send_same(c, first):
        for d in range(first, half):
            @pl.when(d != spot)
            def _():
                c3(c, tier * half + d).start()

    def send_other(c):
        for d in range(half):
            c3(c, other_tier(d)).start()

    @pl.when(tier == 1)
    def _():
        pl.semaphore_wait(barrier, nz + 1)
        for d in range(half):
            greet(late_sem, device(other_tier(d)))

    turn()
    compute(0)

    @pl.when(tier == 0)
    def _():
        pl.semaphore_wait(barrier, half)


    @pl.when(tier == 1)
    def _():
        direct(0)

    c1(0).start()
    for c in range(chunks):
        if c + 1 < chunks:
            compute(c + 1)

            @pl.when(tier == 1)
            def _():
                direct(c + 1)

            c1(c + 1).start()
        encode(c)

        @pl.when(tier == 0)
        def _():
            send_same(c, 0)

        @pl.when(tier == 1)
        def _():
            for d in range(1, half):
                c3(c, d).start()
            send_same(c, 0)

    @pl.when(tier == 0)
    def _():
        pl.semaphore_wait(late_sem, half)
        for c in range(chunks):
            send_other(c)

    others = [lax.rem(z + d, nz) for d in range(1, nz)]

    def number(code):
        return code.astype(jnp.int32).astype(jnp.float32)

    def finish(chips, cores):
        waits = [(r3, chip, r3_wait) for chip in chips] + [(r5, k, r5_wait) for k in range(cores)]
        scales = []
        for c in range(chunks):
            lo, hi = splits[c]
            cols = (hi - lo) * width
            ats = [(at, min(at + LANES, cols)) for at in range(0, cols, LANES)]
            totals = [own[c][z, :, at:end] for at, end in ats]
            for group in ((waits[:-2], waits[-2:]) if c + 1 == chunks else (waits,)):
                for _, src, wait in group:
                    wait(c, src)
                if c == 0:
                    scales = [jnp.exp2(number(r[c][src, :, cols:cols + LANES]) * (-1.0 / 256.0)) for r, src, _ in group]
                used = scales[-2:] if len(group) == 2 else scales[:len(group)]
                for i, (at, end) in enumerate(ats):
                    for (r, src, _), scale in zip(group, used):
                        totals[i] = totals[i] + number(r[c][src, :, at:end]) * scale[:, :end - at]
            for (at, end), total in zip(ats, totals):
                for s in range(lo + at // width, lo + end // width):
                    o_ref[s * t:(s + 1) * t, :] = total[:, (s - lo) * width - at:(s - lo + 1) * width - at]

    @pl.when(z == 0)
    def _():
        finish(list(range(1, half)), nz)

    @pl.when(z != 0)
    def _():
        finish(others, 0)

    for c in range(chunks):
        c1(c).wait_send()

    @pl.when(tier == 0)
    def _():
        for c in range(chunks):
            for chip in others:
                c3(c, chip).wait_send()

    @pl.when(tier == 1)
    def _():
        for c in range(chunks):
            for d in range(1, half):
                c3(c, d).wait_send()
                c3(c, same_tier(d)).wait_send()
            for side in range(2):
                c5(c, side).wait_send()


def unfold(t, v_ref, o_ref, lined):
    width = v_ref.shape[1]
    far = width // 2
    value = jnp.concatenate([v_ref[...], jnp.zeros((width * t - v_ref.shape[0], width), jnp.float32)], axis=0)
    lane = lax.broadcasted_iota(jnp.int32, value.shape, 1)
    step = 1
    while step < width:
        value = jnp.where((lane & step) != 0, jnp.roll(value, step * t, axis=0), value)
        step *= 2
    lined[...] = value
    row = lax.broadcasted_iota(jnp.int32, (width, width), 0)
    col = lax.broadcasted_iota(jnp.int32, (width, width), 1)
    near = within(row - col + width, width) <= far
    for q in range(t):
        at = pl.ds(q, width, stride=t)
        below = lined[at, :]
        lined[at, :] = jnp.where(near, below, below.T)
    per = LANES // width
    for m in range(width // per):
        o_ref[:, m * LANES:(m + 1) * LANES] = jnp.concatenate(
            [lined[(m * per + i) * t:(m * per + i + 1) * t, :] for i in range(per)], axis=1)


def per_device(row_leaves, covariates, query_leaves, leaf_sizes):
    n = lax.axis_size("rows")
    trees, rows = row_leaves.shape
    width = covariates.shape[0]
    queries = query_leaves.shape[1]
    t = queries // n
    nz = n // 2
    sub = nz * t
    cols = [(hi - lo) * width for lo, hi in splits_of(width)]
    chunks = len(cols)
    vmem = pl.BlockSpec(memory_space=pltpu.VMEM)
    f32 = jnp.float32
    i16 = jnp.int16
    dma = pltpu.SemaphoreType.DMA
    folded = pl.pallas_call(
        functools.partial(kernel, n),
        out_shape=pltpu.VMEM(((width // 2 + 1) * t, width), f32),
        in_specs=[pl.BlockSpec(memory_space=pltpu.HBM)] * 4,
        out_specs=vmem,
        scratch_shapes=[
            pltpu.VMEM(row_leaves.shape, jnp.int32),
            pltpu.VMEM(covariates.shape, jnp.bfloat16),
            pltpu.VMEM(query_leaves.shape, jnp.int32),
            pltpu.VMEM(leaf_sizes.shape, jnp.int32),
            pltpu.VMEM((TURNS, width + width // 2, rows), jnp.bfloat16),
            pltpu.VMEM((trees, queries, STEP), i16),
            pltpu.VMEM((trees, queries, STEP), i16),
            pltpu.VMEM((queries, rows), jnp.bfloat16),
            pltpu.VMEM((queries, queries), jnp.bfloat16),
            pltpu.VMEM((trees, trees * LANES), jnp.bfloat16),
            pltpu.VMEM((sub + 2 * t, LANES), f32),
            pltpu.SemaphoreType.REGULAR,
            dma((3,)), dma((rows // (PIECES * STEP),)),
            dma((chunks,)), dma((chunks,)),
            dma((chunks, nz)), dma((chunks, nz)),
            dma((chunks, 2)), dma((chunks, nz)),
            *[pltpu.VMEM((2, sub, c), f32) for c in cols],
            *[pltpu.VMEM((nz, t, c), f32) for c in cols],
            *[pltpu.VMEM((nz, t, coded_width(c)), i16) for c in cols],
            *[pltpu.VMEM((sub, c), f32) for c in cols],
            *[pltpu.VMEM((nz, t, coded_width(c)), i16) for c in cols],
            *[pltpu.VMEM((2, t, coded_width(c)), i16) for c in cols],
            *[pltpu.VMEM((nz, t, coded_width(c)), i16) for c in cols],
        ],
        compiler_params=pltpu.CompilerParams(collective_id=0, has_side_effects=True,
                                             vmem_limit_bytes=56 << 20),
    )(row_leaves, covariates, query_leaves, leaf_sizes)
    return pl.pallas_call(
        functools.partial(unfold, t),
        out_shape=jax.ShapeDtypeStruct((t, width * width), f32),
        in_specs=[vmem],
        out_specs=vmem,
        scratch_shapes=[pltpu.VMEM((width * t, width), f32)],
        compiler_params=pltpu.CompilerParams(vmem_limit_bytes=16 << 20),
    )(folded)


def solution(mesh):
    return jax.shard_map(
        per_device,
        mesh=mesh,
        in_specs=(
            P(None, ("groups", "rows")),
            P(None, ("groups", "rows")),
            P(None, "groups"),
            P("groups", None),
        ),
        out_specs=P(("groups", "rows"), None),
        check_vma=False,
    )
```

```python
import functools

import jax
import jax.numpy as jnp
from jax import lax
from jax.experimental import pallas as pl
from jax.experimental.pallas import tpu as pltpu
from jax.sharding import PartitionSpec as P

LANES = 128
STEP = 256
TURNS = 8
PIECES = 2


def splits_of(width):
    return [(0, width // 4), (width // 4, width // 2 + 1)]


def power_of(value):
    largest = jnp.maximum(jnp.max(jnp.abs(value), axis=1, keepdims=True), 1e-30)
    return jnp.floor(256.0 * jnp.log2(32000.0 / jnp.broadcast_to(largest, (value.shape[0], LANES))))


def coded(value, power):
    scale = jnp.exp2(power * (1.0 / 256.0))
    pieces = []
    for at in range(0, value.shape[1], LANES):
        piece = value[:, at:at + LANES]
        pieces.append(jnp.round(piece * scale[:, :piece.shape[1]]).astype(jnp.int32))
    spare = -value.shape[1] % LANES or LANES
    return jnp.concatenate(pieces + [power[:, :spare].astype(jnp.int32)], axis=1)


def coded_width(cols):
    return cols + (-cols % LANES or LANES)


def over(value, size):
    return value >> (size.bit_length() - 1) if size & (size - 1) == 0 else value // size


def within(value, size):
    return value & (size - 1) if size & (size - 1) == 0 else lax.rem(value, size)


def kernel(n, rl_hbm, x_hbm, ql_hbm, ls_hbm, o_ref, rl, x, ql, ls, turns, qb, wb, w_s, order, spread, powers, late_sem, in_sems, rl_sems,
           ss1, rs1, ss3, rs3, ss5, rs5, *bufs):
    trees, rows = rl.shape
    width = x.shape[0]
    queries = ql.shape[1]
    splits = splits_of(width)
    chunks = len(splits)
    part, own, s3, r1, r3, s5, r5 = (bufs[i * chunks:(i + 1) * chunks] for i in range(7))
    t = queries // n
    nz = n // 2
    half = nz // 2
    sub = nz * t
    me = lax.axis_index("rows")
    core = lax.rem(me, 2)
    z = me // 2
    tier = z // half
    spot = lax.rem(z, half)
    sibling = me + 1 - 2 * core

    def device(chip):
        return chip * 2 + core

    def same_tier(d):
        return tier * half + lax.rem(spot + d, half)

    def other_tier(d):
        return (1 - tier) * half + lax.rem(spot + d, half)

    def greet(sem, peer):
        pl.semaphore_signal(sem, inc=1, device_id={"rows": peer}, device_id_type=pl.DeviceIdType.MESH)

    def rl_copy(step):
        at = pl.ds(pl.multiple_of(step * PIECES * STEP, PIECES * STEP), PIECES * STEP)
        return pltpu.make_async_copy(rl_hbm.at[:, at], rl.at[:, at], rl_sems.at[step])

    ins = [pltpu.make_async_copy(a, b, in_sems.at[i])
           for i, (a, b) in enumerate(((ls_hbm, ls), (ql_hbm, ql), (x_hbm, x)))]
    ins[0].start()
    ins[1].start()
    for step in range(rows // (PIECES * STEP)):
        rl_copy(step).start()
    ins[2].start()

    barrier = pltpu.get_barrier_semaphore()
    greet(barrier, sibling)
    for d in range(1, half):
        greet(barrier, device(same_tier(d)))

    @pl.when(tier == 0)
    def _():
        for d in range(half):
            greet(barrier, device(other_tier(d)))

    @pl.when(z == 0)
    def _():
        for d in range(half):
            greet(barrier, other_tier(d) * 2 + 1 - core)

    bf16 = jnp.bfloat16
    place = lax.broadcasted_iota(jnp.int32, (queries, queries), 0)
    query = lax.broadcasted_iota(jnp.int32, (queries, queries), 1)
    pick = (over(within(place, sub), t) * 2 + over(place, sub)) * t + within(place, t)
    order[...] = jnp.where(query == pick, 1.0, 0.0).astype(bf16)
    tree_of = over(lax.broadcasted_iota(jnp.int32, (trees, trees * LANES), 1), LANES)
    tree_at = lax.broadcasted_iota(jnp.int32, (trees, trees * LANES), 0)
    spread[...] = jnp.where(tree_of == tree_at, 1.0, 0.0).astype(bf16)
    ins[0].wait()
    ins[1].wait()

    units = float(128 * trees * 2 * rows * n // ls.shape[1])
    inverse = 1.0 / (trees * ls[...].astype(jnp.float32))
    chosen = []
    for first in range(0, queries, LANES):
        piece = ql[:, first:first + LANES]
        wide = piece.shape[1]
        if wide < LANES:
            piece = jnp.concatenate([piece] * (LANES // wide), axis=1)
        chosen.append(jnp.take_along_axis(inverse, piece, axis=1)[:, :wide])
    chosen = jnp.concatenate(chosen, axis=1).astype(bf16) * bf16(units)
    both = jnp.concatenate(
        [lax.dot_general(order[...], table, (((1,), (1,)), ((), ())), preferred_element_type=jnp.float32).astype(bf16)
         for table in (ql[...].astype(jnp.float32).astype(bf16), chosen)], axis=0)
    batch = 4
    for first in range(0, trees, batch):
        wide = jnp.dot(both, spread[:, first * LANES:(first + batch) * LANES],
                       preferred_element_type=jnp.float32).astype(jnp.int32)
        for b in range(first, first + batch):
            one = wide[:, (b - first) * LANES:(b - first + 1) * LANES]
            one = jnp.concatenate([one] * (STEP // LANES), axis=1).astype(jnp.int16)
            qb[b] = one[:queries]
            wb[b] = one[queries:]

    tile = 64
    share = 16

    def weights_step(step, carry):
        ats = [pl.ds(pl.multiple_of((step * PIECES + i) * STEP, STEP), STEP) for i in range(PIECES)]
        rl_copy(step).wait()
        for q0 in range(0, queries, tile):
            def tree(b, accs):
                leaf = qb[b, q0:q0 + tile, :]
                weight = wb[b, q0:q0 + tile, :]
                out = []
                for at, acc in zip(ats, accs):
                    row = jnp.broadcast_to(rl[pl.ds(b, 1), at], (8, STEP)).astype(jnp.int16)
                    row = jnp.concatenate([row] * (tile // 8), axis=0)
                    out.append(acc + jnp.where(leaf == row, weight, jnp.zeros_like(weight)))
                return tuple(out)

            accs = lax.fori_loop(0, trees, tree, (jnp.zeros((tile, STEP), jnp.int16),) * PIECES, unroll=share)
            for at, acc in zip(ats, accs):
                total = acc.astype(jnp.int32).astype(jnp.float32) * (1.0 / units)
                w_s[q0:q0 + tile, at] = total.astype(jnp.bfloat16)
        return carry

    lax.fori_loop(0, rows // (STEP * PIECES), weights_step, 0)
    ins[2].wait()
    def turn():
        for at in range(0, rows, 2 * STEP):
            wide = x[:, at:at + 2 * STEP].astype(jnp.float32)
            for r in range(TURNS):
                turned = (jnp.roll(wide, -r, axis=0) if r else wide).astype(bf16)
                turns[r, :width, at:at + 2 * STEP] = turned
                turns[r, width:, at:at + 2 * STEP] = turned[:turns.shape[1] - width]

    def compute(c):
        lo, hi = splits[c]
        per = STEP // width
        for s in range(lo, hi, per):
            ends = min(hi, s + per)
            prod = jnp.concatenate(
                [x[...] * turns[e % TURNS, e // TURNS * TURNS:e // TURNS * TURNS + width, :] for e in range(s, ends)], axis=0)
            res = lax.dot_general(prod, w_s[...], (((1,), (1,)), ((), ())), preferred_element_type=jnp.float32).T
            for a in range(2):
                part[c][a, :, (s - lo) * width:(ends - lo) * width] = res[a * sub:(a + 1) * sub, :]

    def copy(src, dst, ssem, rsem, peer):
        return pltpu.make_async_remote_copy(src_ref=src, dst_ref=dst, send_sem=ssem, recv_sem=rsem,
                                            device_id={"rows": peer}, device_id_type=pl.DeviceIdType.MESH)

    def c1(c):
        return copy(part[c].at[1 - core], r1[c], ss1.at[c], rs1.at[c], sibling)

    def c3(c, chip):
        return copy(s3[c].at[chip], r3[c].at[z], ss3.at[c, chip], rs3.at[c, z], device(chip))

    def r3_wait(c, chip):
        copy(s3[c].at[chip], r3[c].at[chip], ss3.at[c, chip], rs3.at[c, chip], device(chip)).wait_recv()

    def encode(c):
        c1(c).wait_recv()
        total = part[c][core] + r1[c][...]
        if c == 0:
            power = power_of(total[:, :width])
            powers[:sub] = power
        else:
            power = powers[:sub]
        code = coded(total, power)
        for k in range(nz):
            own[c][k] = total[k * t:(k + 1) * t, :]
            s3[c][k] = code[k * t:(k + 1) * t, :].astype(jnp.int16)

    def c5(c, side):
        return copy(s5[c].at[side], r5[c].at[me - nz], ss5.at[c, side], rs5.at[c, me - nz], side)

    def r5_wait(c, k):
        copy(s5[c].at[0], r5[c].at[k], ss5.at[c, 0], rs5.at[c, k], nz + k).wait_recv()

    def direct(c):
        value = jnp.concatenate([part[c][a][:t, :] for a in range(2)], axis=0)
        if c == 0:
            power = power_of(value[:, :width])
            powers[sub:] = power
        else:
            power = powers[sub:]
        code = coded(value, power)
        for a in range(2):
            s5[c][a] = code[a * t:(a + 1) * t, :].astype(jnp.int16)
            c5(c, a).start()

    def send_same(c, first):
        for d in range(first, half):
            @pl.when(d != spot)
            def _():
                c3(c, tier * half + d).start()

    def send_other(c):
        for d in range(half):
            c3(c, other_tier(d)).start()

    @pl.when(tier == 1)
    def _():
        pl.semaphore_wait(barrier, nz + 1)
        for d in range(half):
            greet(late_sem, device(other_tier(d)))

    turn()
    compute(0)

    @pl.when(tier == 0)
    def _():
        pl.semaphore_wait(barrier, half)


    @pl.when(tier == 1)
    def _():
        direct(0)

    c1(0).start()
    for c in range(chunks):
        if c + 1 < chunks:
            compute(c + 1)

            @pl.when(tier == 1)
            def _():
                direct(c + 1)

            c1(c + 1).start()
        encode(c)

        @pl.when(tier == 0)
        def _():
            send_same(c, 0)

        @pl.when(tier == 1)
        def _():
            for d in range(1, half):
                c3(c, d).start()
            if c + 1 == chunks:
                for k in range(chunks):
                    send_same(k, 0)

    @pl.when(tier == 0)
    def _():
        pl.semaphore_wait(late_sem, half)
        for c in range(chunks):
            send_other(c)

    others = [lax.rem(z + d, nz) for d in range(1, nz)]

    def number(code):
        return code.astype(jnp.int32).astype(jnp.float32)

    def finish(chips, cores):
        waits = [(r3, chip, r3_wait) for chip in chips] + [(r5, k, r5_wait) for k in range(cores)]
        scales = []
        for c in range(chunks):
            lo, hi = splits[c]
            cols = (hi - lo) * width
            ats = [(at, min(at + LANES, cols)) for at in range(0, cols, LANES)]
            totals = [own[c][z, :, at:end] for at, end in ats]
            for group in ((waits[:-2], waits[-2:]) if c + 1 == chunks else (waits,)):
                for _, src, wait in group:
                    wait(c, src)
                if c == 0:
                    scales = [jnp.exp2(number(r[c][src, :, cols:cols + LANES]) * (-1.0 / 256.0)) for r, src, _ in group]
                used = scales[-2:] if len(group) == 2 else scales[:len(group)]
                for i, (at, end) in enumerate(ats):
                    for (r, src, _), scale in zip(group, used):
                        totals[i] = totals[i] + number(r[c][src, :, at:end]) * scale[:, :end - at]
            for (at, end), total in zip(ats, totals):
                for s in range(lo + at // width, lo + end // width):
                    o_ref[s * t:(s + 1) * t, :] = total[:, (s - lo) * width - at:(s - lo + 1) * width - at]

    @pl.when(z == 0)
    def _():
        finish(list(range(1, half)), nz)

    @pl.when(z != 0)
    def _():
        finish(others, 0)

    for c in range(chunks):
        c1(c).wait_send()

    @pl.when(tier == 0)
    def _():
        for c in range(chunks):
            for chip in others:
                c3(c, chip).wait_send()

    @pl.when(tier == 1)
    def _():
        for c in range(chunks):
            for d in range(1, half):
                c3(c, d).wait_send()
                c3(c, same_tier(d)).wait_send()
            for side in range(2):
                c5(c, side).wait_send()


def unfold(t, v_ref, o_ref, lined):
    width = v_ref.shape[1]
    far = width // 2
    value = jnp.concatenate([v_ref[...], jnp.zeros((width * t - v_ref.shape[0], width), jnp.float32)], axis=0)
    lane = lax.broadcasted_iota(jnp.int32, value.shape, 1)
    step = 1
    while step < width:
        value = jnp.where((lane & step) != 0, jnp.roll(value, step * t, axis=0), value)
        step *= 2
    lined[...] = value
    row = lax.broadcasted_iota(jnp.int32, (width, width), 0)
    col = lax.broadcasted_iota(jnp.int32, (width, width), 1)
    near = within(row - col + width, width) <= far
    for q in range(t):
        at = pl.ds(q, width, stride=t)
        below = lined[at, :]
        lined[at, :] = jnp.where(near, below, below.T)
    per = LANES // width
    for m in range(width // per):
        o_ref[:, m * LANES:(m + 1) * LANES] = jnp.concatenate(
            [lined[(m * per + i) * t:(m * per + i + 1) * t, :] for i in range(per)], axis=1)


def per_device(row_leaves, covariates, query_leaves, leaf_sizes):
    n = lax.axis_size("rows")
    trees, rows = row_leaves.shape
    width = covariates.shape[0]
    queries = query_leaves.shape[1]
    t = queries // n
    nz = n // 2
    sub = nz * t
    cols = [(hi - lo) * width for lo, hi in splits_of(width)]
    chunks = len(cols)
    vmem = pl.BlockSpec(memory_space=pltpu.VMEM)
    f32 = jnp.float32
    i16 = jnp.int16
    dma = pltpu.SemaphoreType.DMA
    folded = pl.pallas_call(
        functools.partial(kernel, n),
        out_shape=pltpu.VMEM(((width // 2 + 1) * t, width), f32),
        in_specs=[pl.BlockSpec(memory_space=pltpu.HBM)] * 4,
        out_specs=vmem,
        scratch_shapes=[
            pltpu.VMEM(row_leaves.shape, jnp.int32),
            pltpu.VMEM(covariates.shape, jnp.bfloat16),
            pltpu.VMEM(query_leaves.shape, jnp.int32),
            pltpu.VMEM(leaf_sizes.shape, jnp.int32),
            pltpu.VMEM((TURNS, width + width // 2, rows), jnp.bfloat16),
            pltpu.VMEM((trees, queries, STEP), i16),
            pltpu.VMEM((trees, queries, STEP), i16),
            pltpu.VMEM((queries, rows), jnp.bfloat16),
            pltpu.VMEM((queries, queries), jnp.bfloat16),
            pltpu.VMEM((trees, trees * LANES), jnp.bfloat16),
            pltpu.VMEM((sub + 2 * t, LANES), f32),
            pltpu.SemaphoreType.REGULAR,
            dma((3,)), dma((rows // (PIECES * STEP),)),
            dma((chunks,)), dma((chunks,)),
            dma((chunks, nz)), dma((chunks, nz)),
            dma((chunks, 2)), dma((chunks, nz)),
            *[pltpu.VMEM((2, sub, c), f32) for c in cols],
            *[pltpu.VMEM((nz, t, c), f32) for c in cols],
            *[pltpu.VMEM((nz, t, coded_width(c)), i16) for c in cols],
            *[pltpu.VMEM((sub, c), f32) for c in cols],
            *[pltpu.VMEM((nz, t, coded_width(c)), i16) for c in cols],
            *[pltpu.VMEM((2, t, coded_width(c)), i16) for c in cols],
            *[pltpu.VMEM((nz, t, coded_width(c)), i16) for c in cols],
        ],
        compiler_params=pltpu.CompilerParams(collective_id=0, has_side_effects=True,
                                             vmem_limit_bytes=56 << 20),
    )(row_leaves, covariates, query_leaves, leaf_sizes)
    return pl.pallas_call(
        functools.partial(unfold, t),
        out_shape=jax.ShapeDtypeStruct((t, width * width), f32),
        in_specs=[vmem],
        out_specs=vmem,
        scratch_shapes=[pltpu.VMEM((width * t, width), f32)],
        compiler_params=pltpu.CompilerParams(vmem_limit_bytes=16 << 20),
    )(folded)


def solution(mesh):
    return jax.shard_map(
        per_device,
        mesh=mesh,
        in_specs=(
            P(None, ("groups", "rows")),
            P(None, ("groups", "rows")),
            P(None, "groups"),
            P("groups", None),
        ),
        out_specs=P(("groups", "rows"), None),
        check_vma=False,
    )
```

```python
import functools

import jax
import jax.numpy as jnp
from jax import lax
from jax.experimental import pallas as pl
from jax.experimental.pallas import tpu as pltpu
from jax.sharding import PartitionSpec as P

LANES = 128
STEP = 256
TURNS = 8
PIECES = 4


def splits_of(width):
    return [(0, width // 4), (width // 4, width // 2 + 1)]


def power_of(value):
    largest = jnp.maximum(jnp.max(jnp.abs(value), axis=1, keepdims=True), 1e-30)
    return jnp.floor(256.0 * jnp.log2(32000.0 / jnp.broadcast_to(largest, (value.shape[0], LANES))))


def coded(value, power):
    scale = jnp.exp2(power * (1.0 / 256.0))
    pieces = []
    for at in range(0, value.shape[1], LANES):
        piece = value[:, at:at + LANES]
        pieces.append(jnp.round(piece * scale[:, :piece.shape[1]]).astype(jnp.int32))
    spare = -value.shape[1] % LANES or LANES
    return jnp.concatenate(pieces + [power[:, :spare].astype(jnp.int32)], axis=1)


def coded_width(cols):
    return cols + (-cols % LANES or LANES)


def over(value, size):
    return value >> (size.bit_length() - 1) if size & (size - 1) == 0 else value // size


def within(value, size):
    return value & (size - 1) if size & (size - 1) == 0 else lax.rem(value, size)


def kernel(n, rl_hbm, x_hbm, ql_hbm, ls_hbm, o_ref, rl, x, ql, ls, turns, qb, wb, w_s, order, spread, powers, late_sem, in_sems, rl_sems,
           ss1, rs1, ss3, rs3, ss5, rs5, *bufs):
    trees, rows = rl.shape
    width = x.shape[0]
    queries = ql.shape[1]
    splits = splits_of(width)
    chunks = len(splits)
    part, own, s3, r1, r3, s5, r5 = (bufs[i * chunks:(i + 1) * chunks] for i in range(7))
    t = queries // n
    nz = n // 2
    half = nz // 2
    sub = nz * t
    me = lax.axis_index("rows")
    core = lax.rem(me, 2)
    z = me // 2
    tier = z // half
    spot = lax.rem(z, half)
    sibling = me + 1 - 2 * core

    def device(chip):
        return chip * 2 + core

    def same_tier(d):
        return tier * half + lax.rem(spot + d, half)

    def other_tier(d):
        return (1 - tier) * half + lax.rem(spot + d, half)

    def greet(sem, peer):
        pl.semaphore_signal(sem, inc=1, device_id={"rows": peer}, device_id_type=pl.DeviceIdType.MESH)

    def rl_copy(step):
        at = pl.ds(pl.multiple_of(step * PIECES * STEP, PIECES * STEP), PIECES * STEP)
        return pltpu.make_async_copy(rl_hbm.at[:, at], rl.at[:, at], rl_sems.at[step])

    ins = [pltpu.make_async_copy(a, b, in_sems.at[i])
           for i, (a, b) in enumerate(((ls_hbm, ls), (ql_hbm, ql), (x_hbm, x)))]
    ins[0].start()
    ins[1].start()
    for step in range(rows // (PIECES * STEP)):
        rl_copy(step).start()
    ins[2].start()

    barrier = pltpu.get_barrier_semaphore()
    greet(barrier, sibling)
    for d in range(1, half):
        greet(barrier, device(same_tier(d)))

    @pl.when(tier == 0)
    def _():
        for d in range(half):
            greet(barrier, device(other_tier(d)))

    @pl.when(z == 0)
    def _():
        for d in range(half):
            greet(barrier, other_tier(d) * 2 + 1 - core)

    bf16 = jnp.bfloat16
    place = lax.broadcasted_iota(jnp.int32, (queries, queries), 0)
    query = lax.broadcasted_iota(jnp.int32, (queries, queries), 1)
    pick = (over(within(place, sub), t) * 2 + over(place, sub)) * t + within(place, t)
    order[...] = jnp.where(query == pick, 1.0, 0.0).astype(bf16)
    tree_of = over(lax.broadcasted_iota(jnp.int32, (trees, trees * LANES), 1), LANES)
    tree_at = lax.broadcasted_iota(jnp.int32, (trees, trees * LANES), 0)
    spread[...] = jnp.where(tree_of == tree_at, 1.0, 0.0).astype(bf16)
    ins[0].wait()
    ins[1].wait()

    units = float(128 * trees * 2 * rows * n // ls.shape[1])
    inverse = 1.0 / (trees * ls[...].astype(jnp.float32))
    chosen = []
    for first in range(0, queries, LANES):
        piece = ql[:, first:first + LANES]
        wide = piece.shape[1]
        if wide < LANES:
            piece = jnp.concatenate([piece] * (LANES // wide), axis=1)
        chosen.append(jnp.take_along_axis(inverse, piece, axis=1)[:, :wide])
    chosen = jnp.concatenate(chosen, axis=1).astype(bf16) * bf16(units)
    both = jnp.concatenate(
        [lax.dot_general(order[...], table, (((1,), (1,)), ((), ())), preferred_element_type=jnp.float32).astype(bf16)
         for table in (ql[...].astype(jnp.float32).astype(bf16), chosen)], axis=0)
    batch = 4
    for first in range(0, trees, batch):
        wide = jnp.dot(both, spread[:, first * LANES:(first + batch) * LANES],
                       preferred_element_type=jnp.float32).astype(jnp.int32)
        for b in range(first, first + batch):
            one = wide[:, (b - first) * LANES:(b - first + 1) * LANES]
            one = jnp.concatenate([one] * (STEP // LANES), axis=1).astype(jnp.int16)
            qb[b] = one[:queries]
            wb[b] = one[queries:]

    tile = 32
    share = 8

    def weights_step(step, carry):
        ats = [pl.ds(pl.multiple_of((step * PIECES + i) * STEP, STEP), STEP) for i in range(PIECES)]
        rl_copy(step).wait()
        for q0 in range(0, queries, tile):
            def tree(b, accs):
                leaf = qb[b, q0:q0 + tile, :]
                weight = wb[b, q0:q0 + tile, :]
                out = []
                for at, acc in zip(ats, accs):
                    row = jnp.broadcast_to(rl[pl.ds(b, 1), at], (8, STEP)).astype(jnp.int16)
                    row = jnp.concatenate([row] * (tile // 8), axis=0)
                    out.append(acc + jnp.where(leaf == row, weight, jnp.zeros_like(weight)))
                return tuple(out)

            accs = lax.fori_loop(0, trees, tree, (jnp.zeros((tile, STEP), jnp.int16),) * PIECES, unroll=share)
            for at, acc in zip(ats, accs):
                total = acc.astype(jnp.int32).astype(jnp.float32) * (1.0 / units)
                w_s[q0:q0 + tile, at] = total.astype(jnp.bfloat16)
        return carry

    lax.fori_loop(0, rows // (STEP * PIECES), weights_step, 0)
    ins[2].wait()
    def turn():
        for at in range(0, rows, 2 * STEP):
            wide = x[:, at:at + 2 * STEP].astype(jnp.float32)
            for r in range(TURNS):
                turned = (jnp.roll(wide, -r, axis=0) if r else wide).astype(bf16)
                turns[r, :width, at:at + 2 * STEP] = turned
                turns[r, width:, at:at + 2 * STEP] = turned[:turns.shape[1] - width]

    def compute(c):
        lo, hi = splits[c]
        per = STEP // width
        for s in range(lo, hi, per):
            ends = min(hi, s + per)
            prod = jnp.concatenate(
                [x[...] * turns[e % TURNS, e // TURNS * TURNS:e // TURNS * TURNS + width, :] for e in range(s, ends)], axis=0)
            res = lax.dot_general(prod, w_s[...], (((1,), (1,)), ((), ())), preferred_element_type=jnp.float32).T
            for a in range(2):
                part[c][a, :, (s - lo) * width:(ends - lo) * width] = res[a * sub:(a + 1) * sub, :]

    def copy(src, dst, ssem, rsem, peer):
        return pltpu.make_async_remote_copy(src_ref=src, dst_ref=dst, send_sem=ssem, recv_sem=rsem,
                                            device_id={"rows": peer}, device_id_type=pl.DeviceIdType.MESH)

    def c1(c):
        return copy(part[c].at[1 - core], r1[c], ss1.at[c], rs1.at[c], sibling)

    def c3(c, chip):
        return copy(s3[c].at[chip], r3[c].at[z], ss3.at[c, chip], rs3.at[c, z], device(chip))

    def r3_wait(c, chip):
        copy(s3[c].at[chip], r3[c].at[chip], ss3.at[c, chip], rs3.at[c, chip], device(chip)).wait_recv()

    def encode(c):
        c1(c).wait_recv()
        total = part[c][core] + r1[c][...]
        if c == 0:
            power = power_of(total[:, :width])
            powers[:sub] = power
        else:
            power = powers[:sub]
        code = coded(total, power)
        for k in range(nz):
            own[c][k] = total[k * t:(k + 1) * t, :]
            s3[c][k] = code[k * t:(k + 1) * t, :].astype(jnp.int16)

    def c5(c, side):
        return copy(s5[c].at[side], r5[c].at[me - nz], ss5.at[c, side], rs5.at[c, me - nz], side)

    def r5_wait(c, k):
        copy(s5[c].at[0], r5[c].at[k], ss5.at[c, 0], rs5.at[c, k], nz + k).wait_recv()

    def direct(c):
        value = jnp.concatenate([part[c][a][:t, :] for a in range(2)], axis=0)
        if c == 0:
            power = power_of(value[:, :width])
            powers[sub:] = power
        else:
            power = powers[sub:]
        code = coded(value, power)
        for a in range(2):
            s5[c][a] = code[a * t:(a + 1) * t, :].astype(jnp.int16)
            c5(c, a).start()

    def send_same(c, first):
        for d in range(first, half):
            @pl.when(d != spot)
            def _():
                c3(c, tier * half + d).start()

    def send_other(c):
        for d in range(half):
            c3(c, other_tier(d)).start()

    @pl.when(tier == 1)
    def _():
        pl.semaphore_wait(barrier, nz + 1)
        for d in range(half):
            greet(late_sem, device(other_tier(d)))

    turn()
    compute(0)

    @pl.when(tier == 0)
    def _():
        pl.semaphore_wait(barrier, half)


    @pl.when(tier == 1)
    def _():
        direct(0)

    c1(0).start()
    for c in range(chunks):
        if c + 1 < chunks:
            compute(c + 1)

            @pl.when(tier == 1)
            def _():
                direct(c + 1)

            c1(c + 1).start()
        encode(c)

        @pl.when(tier == 0)
        def _():
            send_same(c, 0)

        @pl.when(tier == 1)
        def _():
            for d in range(1, half):
                c3(c, d).start()
            if c + 1 == chunks:
                for k in range(chunks):
                    send_same(k, 0)

    @pl.when(tier == 0)
    def _():
        pl.semaphore_wait(late_sem, half)
        for c in range(chunks):
            send_other(c)

    others = [lax.rem(z + d, nz) for d in range(1, nz)]

    def number(code):
        return code.astype(jnp.int32).astype(jnp.float32)

    def finish(chips, cores):
        waits = [(r3, chip, r3_wait) for chip in chips] + [(r5, k, r5_wait) for k in range(cores)]
        scales = []
        for c in range(chunks):
            lo, hi = splits[c]
            cols = (hi - lo) * width
            ats = [(at, min(at + LANES, cols)) for at in range(0, cols, LANES)]
            totals = [own[c][z, :, at:end] for at, end in ats]
            for group in ((waits[:-2], waits[-2:]) if c + 1 == chunks else (waits,)):
                for _, src, wait in group:
                    wait(c, src)
                if c == 0:
                    scales = [jnp.exp2(number(r[c][src, :, cols:cols + LANES]) * (-1.0 / 256.0)) for r, src, _ in group]
                used = scales[-2:] if len(group) == 2 else scales[:len(group)]
                for i, (at, end) in enumerate(ats):
                    for (r, src, _), scale in zip(group, used):
                        totals[i] = totals[i] + number(r[c][src, :, at:end]) * scale[:, :end - at]
            for (at, end), total in zip(ats, totals):
                for s in range(lo + at // width, lo + end // width):
                    o_ref[s * t:(s + 1) * t, :] = total[:, (s - lo) * width - at:(s - lo + 1) * width - at]

    @pl.when(z == 0)
    def _():
        finish(list(range(1, half)), nz)

    @pl.when(z != 0)
    def _():
        finish(others, 0)

    for c in range(chunks):
        c1(c).wait_send()

    @pl.when(tier == 0)
    def _():
        for c in range(chunks):
            for chip in others:
                c3(c, chip).wait_send()

    @pl.when(tier == 1)
    def _():
        for c in range(chunks):
            for d in range(1, half):
                c3(c, d).wait_send()
                c3(c, same_tier(d)).wait_send()
            for side in range(2):
                c5(c, side).wait_send()


def unfold(t, v_ref, o_ref, lined):
    width = v_ref.shape[1]
    far = width // 2
    value = jnp.concatenate([v_ref[...], jnp.zeros((width * t - v_ref.shape[0], width), jnp.float32)], axis=0)
    lane = lax.broadcasted_iota(jnp.int32, value.shape, 1)
    step = 1
    while step < width:
        value = jnp.where((lane & step) != 0, jnp.roll(value, step * t, axis=0), value)
        step *= 2
    lined[...] = value
    row = lax.broadcasted_iota(jnp.int32, (width, width), 0)
    col = lax.broadcasted_iota(jnp.int32, (width, width), 1)
    near = within(row - col + width, width) <= far
    for q in range(t):
        at = pl.ds(q, width, stride=t)
        below = lined[at, :]
        lined[at, :] = jnp.where(near, below, below.T)
    per = LANES // width
    for m in range(width // per):
        o_ref[:, m * LANES:(m + 1) * LANES] = jnp.concatenate(
            [lined[(m * per + i) * t:(m * per + i + 1) * t, :] for i in range(per)], axis=1)


def per_device(row_leaves, covariates, query_leaves, leaf_sizes):
    n = lax.axis_size("rows")
    trees, rows = row_leaves.shape
    width = covariates.shape[0]
    queries = query_leaves.shape[1]
    t = queries // n
    nz = n // 2
    sub = nz * t
    cols = [(hi - lo) * width for lo, hi in splits_of(width)]
    chunks = len(cols)
    vmem = pl.BlockSpec(memory_space=pltpu.VMEM)
    f32 = jnp.float32
    i16 = jnp.int16
    dma = pltpu.SemaphoreType.DMA
    folded = pl.pallas_call(
        functools.partial(kernel, n),
        out_shape=pltpu.VMEM(((width // 2 + 1) * t, width), f32),
        in_specs=[pl.BlockSpec(memory_space=pltpu.HBM)] * 4,
        out_specs=vmem,
        scratch_shapes=[
            pltpu.VMEM(row_leaves.shape, jnp.int32),
            pltpu.VMEM(covariates.shape, jnp.bfloat16),
            pltpu.VMEM(query_leaves.shape, jnp.int32),
            pltpu.VMEM(leaf_sizes.shape, jnp.int32),
            pltpu.VMEM((TURNS, width + width // 2, rows), jnp.bfloat16),
            pltpu.VMEM((trees, queries, STEP), i16),
            pltpu.VMEM((trees, queries, STEP), i16),
            pltpu.VMEM((queries, rows), jnp.bfloat16),
            pltpu.VMEM((queries, queries), jnp.bfloat16),
            pltpu.VMEM((trees, trees * LANES), jnp.bfloat16),
            pltpu.VMEM((sub + 2 * t, LANES), f32),
            pltpu.SemaphoreType.REGULAR,
            dma((3,)), dma((rows // (PIECES * STEP),)),
            dma((chunks,)), dma((chunks,)),
            dma((chunks, nz)), dma((chunks, nz)),
            dma((chunks, 2)), dma((chunks, nz)),
            *[pltpu.VMEM((2, sub, c), f32) for c in cols],
            *[pltpu.VMEM((nz, t, c), f32) for c in cols],
            *[pltpu.VMEM((nz, t, coded_width(c)), i16) for c in cols],
            *[pltpu.VMEM((sub, c), f32) for c in cols],
            *[pltpu.VMEM((nz, t, coded_width(c)), i16) for c in cols],
            *[pltpu.VMEM((2, t, coded_width(c)), i16) for c in cols],
            *[pltpu.VMEM((nz, t, coded_width(c)), i16) for c in cols],
        ],
        compiler_params=pltpu.CompilerParams(collective_id=0, has_side_effects=True,
                                             vmem_limit_bytes=56 << 20),
    )(row_leaves, covariates, query_leaves, leaf_sizes)
    return pl.pallas_call(
        functools.partial(unfold, t),
        out_shape=jax.ShapeDtypeStruct((t, width * width), f32),
        in_specs=[vmem],
        out_specs=vmem,
        scratch_shapes=[pltpu.VMEM((width * t, width), f32)],
        compiler_params=pltpu.CompilerParams(vmem_limit_bytes=16 << 20),
    )(folded)


def solution(mesh):
    return jax.shard_map(
        per_device,
        mesh=mesh,
        in_specs=(
            P(None, ("groups", "rows")),
            P(None, ("groups", "rows")),
            P(None, "groups"),
            P("groups", None),
        ),
        out_specs=P(("groups", "rows"), None),
        check_vma=False,
    )
```

```python
import functools

import jax
import jax.numpy as jnp
from jax import lax
from jax.experimental import pallas as pl
from jax.experimental.pallas import tpu as pltpu
from jax.sharding import PartitionSpec as P

LANES = 128
STEP = 256
TURNS = 8
PIECES = 2


def splits_of(width):
    return [(0, width // 4), (width // 4, width // 2 + 1)]


def power_of(value):
    largest = jnp.maximum(jnp.max(jnp.abs(value), axis=1, keepdims=True), 1e-30)
    return jnp.floor(256.0 * jnp.log2(32000.0 / jnp.broadcast_to(largest, (value.shape[0], LANES))))


def coded(value, power):
    scale = jnp.exp2(power * (1.0 / 256.0))
    pieces = []
    for at in range(0, value.shape[1], LANES):
        piece = value[:, at:at + LANES]
        pieces.append(jnp.round(piece * scale[:, :piece.shape[1]]).astype(jnp.int32))
    spare = -value.shape[1] % LANES or LANES
    return jnp.concatenate(pieces + [power[:, :spare].astype(jnp.int32)], axis=1)


def coded_width(cols):
    return cols + (-cols % LANES or LANES)


def over(value, size):
    return value >> (size.bit_length() - 1) if size & (size - 1) == 0 else value // size


def within(value, size):
    return value & (size - 1) if size & (size - 1) == 0 else lax.rem(value, size)


def kernel(n, rl_hbm, x_hbm, ql_hbm, ls_hbm, o_ref, rl, x, ql, ls, turns, qb, wb, w_s, order, spread, powers, late_sem, in_sems, rl_sems,
           ss1, rs1, ss3, rs3, ss5, rs5, *bufs):
    trees, rows = rl.shape
    width = x.shape[0]
    queries = ql.shape[1]
    splits = splits_of(width)
    chunks = len(splits)
    part, own, s3, r1, r3, s5, r5 = (bufs[i * chunks:(i + 1) * chunks] for i in range(7))
    t = queries // n
    nz = n // 2
    half = nz // 2
    sub = nz * t
    me = lax.axis_index("rows")
    core = lax.rem(me, 2)
    z = me // 2
    tier = z // half
    spot = lax.rem(z, half)
    sibling = me + 1 - 2 * core

    def device(chip):
        return chip * 2 + core

    def same_tier(d):
        return tier * half + lax.rem(spot + d, half)

    def other_tier(d):
        return (1 - tier) * half + lax.rem(spot + d, half)

    def greet(sem, peer):
        pl.semaphore_signal(sem, inc=1, device_id={"rows": peer}, device_id_type=pl.DeviceIdType.MESH)

    def rl_copy(step):
        at = pl.ds(pl.multiple_of(step * PIECES * STEP, PIECES * STEP), PIECES * STEP)
        return pltpu.make_async_copy(rl_hbm.at[:, at], rl.at[:, at], rl_sems.at[step])

    ins = [pltpu.make_async_copy(a, b, in_sems.at[i])
           for i, (a, b) in enumerate(((ls_hbm, ls), (ql_hbm, ql), (x_hbm, x)))]
    ins[1].start()
    ins[0].start()
    rl_copy(0).start()
    ins[2].start()
    for step in range(1, rows // (PIECES * STEP)):
        rl_copy(step).start()

    barrier = pltpu.get_barrier_semaphore()
    greet(barrier, sibling)
    for d in range(1, half):
        greet(barrier, device(same_tier(d)))

    @pl.when(tier == 0)
    def _():
        for d in range(half):
            greet(barrier, device(other_tier(d)))

    @pl.when(z == 0)
    def _():
        for d in range(half):
            greet(barrier, other_tier(d) * 2 + 1 - core)

    bf16 = jnp.bfloat16
    place = lax.broadcasted_iota(jnp.int32, (queries, queries), 0)
    query = lax.broadcasted_iota(jnp.int32, (queries, queries), 1)
    pick = (over(within(place, sub), t) * 2 + over(place, sub)) * t + within(place, t)
    order[...] = jnp.where(query == pick, 1.0, 0.0).astype(bf16)
    tree_of = over(lax.broadcasted_iota(jnp.int32, (trees, trees * LANES), 1), LANES)
    tree_at = lax.broadcasted_iota(jnp.int32, (trees, trees * LANES), 0)
    spread[...] = jnp.where(tree_of == tree_at, 1.0, 0.0).astype(bf16)
    ins[0].wait()
    ins[1].wait()

    units = float(128 * trees * 2 * rows * n // ls.shape[1])
    inverse = 1.0 / (trees * ls[...].astype(jnp.float32))
    chosen = []
    for first in range(0, queries, LANES):
        piece = ql[:, first:first + LANES]
        wide = piece.shape[1]
        if wide < LANES:
            piece = jnp.concatenate([piece] * (LANES // wide), axis=1)
        chosen.append(jnp.take_along_axis(inverse, piece, axis=1)[:, :wide])
    chosen = jnp.concatenate(chosen, axis=1).astype(bf16) * bf16(units)
    both = jnp.concatenate(
        [lax.dot_general(order[...], table, (((1,), (1,)), ((), ())), preferred_element_type=jnp.float32).astype(bf16)
         for table in (ql[...].astype(jnp.float32).astype(bf16), chosen)], axis=0)
    batch = 4
    for first in range(0, trees, batch):
        wide = jnp.dot(both, spread[:, first * LANES:(first + batch) * LANES],
                       preferred_element_type=jnp.float32).astype(jnp.int32)
        for b in range(first, first + batch):
            one = wide[:, (b - first) * LANES:(b - first + 1) * LANES]
            one = jnp.concatenate([one] * (STEP // LANES), axis=1).astype(jnp.int16)
            qb[b] = one[:queries]
            wb[b] = one[queries:]

    tile = 64
    share = 16

    def weights_step(step, carry):
        ats = [pl.ds(pl.multiple_of((step * PIECES + i) * STEP, STEP), STEP) for i in range(PIECES)]
        rl_copy(step).wait()
        for q0 in range(0, queries, tile):
            def tree(b, accs):
                leaf = qb[b, q0:q0 + tile, :]
                weight = wb[b, q0:q0 + tile, :]
                out = []
                for at, acc in zip(ats, accs):
                    row = jnp.broadcast_to(rl[pl.ds(b, 1), at], (8, STEP)).astype(jnp.int16)
                    row = jnp.concatenate([row] * (tile // 8), axis=0)
                    out.append(acc + jnp.where(leaf == row, weight, jnp.zeros_like(weight)))
                return tuple(out)

            accs = lax.fori_loop(0, trees, tree, (jnp.zeros((tile, STEP), jnp.int16),) * PIECES, unroll=share)
            for at, acc in zip(ats, accs):
                total = acc.astype(jnp.int32).astype(jnp.float32) * (1.0 / units)
                w_s[q0:q0 + tile, at] = total.astype(jnp.bfloat16)
        return carry

    lax.fori_loop(0, rows // (STEP * PIECES), weights_step, 0)
    ins[2].wait()
    def turn():
        for at in range(0, rows, 2 * STEP):
            wide = x[:, at:at + 2 * STEP].astype(jnp.float32)
            for r in range(TURNS):
                turned = (jnp.roll(wide, -r, axis=0) if r else wide).astype(bf16)
                turns[r, :width, at:at + 2 * STEP] = turned
                turns[r, width:, at:at + 2 * STEP] = turned[:turns.shape[1] - width]

    def compute(c):
        lo, hi = splits[c]
        per = STEP // width
        for s in range(lo, hi, per):
            ends = min(hi, s + per)
            prod = jnp.concatenate(
                [x[...] * turns[e % TURNS, e // TURNS * TURNS:e // TURNS * TURNS + width, :] for e in range(s, ends)], axis=0)
            res = lax.dot_general(prod, w_s[...], (((1,), (1,)), ((), ())), preferred_element_type=jnp.float32).T
            for a in range(2):
                part[c][a, :, (s - lo) * width:(ends - lo) * width] = res[a * sub:(a + 1) * sub, :]

    def copy(src, dst, ssem, rsem, peer):
        return pltpu.make_async_remote_copy(src_ref=src, dst_ref=dst, send_sem=ssem, recv_sem=rsem,
                                            device_id={"rows": peer}, device_id_type=pl.DeviceIdType.MESH)

    def c1(c):
        return copy(part[c].at[1 - core], r1[c], ss1.at[c], rs1.at[c], sibling)

    def c3(c, chip):
        return copy(s3[c].at[chip], r3[c].at[z], ss3.at[c, chip], rs3.at[c, z], device(chip))

    def r3_wait(c, chip):
        copy(s3[c].at[chip], r3[c].at[chip], ss3.at[c, chip], rs3.at[c, chip], device(chip)).wait_recv()

    def encode(c):
        c1(c).wait_recv()
        total = part[c][core] + r1[c][...]
        if c == 0:
            power = power_of(total[:, :width])
            powers[:sub] = power
        else:
            power = powers[:sub]
        code = coded(total, power)
        for k in range(nz):
            own[c][k] = total[k * t:(k + 1) * t, :]
            s3[c][k] = code[k * t:(k + 1) * t, :].astype(jnp.int16)

    def c5(c, side):
        return copy(s5[c].at[side], r5[c].at[me - nz], ss5.at[c, side], rs5.at[c, me - nz], side)

    def r5_wait(c, k):
        copy(s5[c].at[0], r5[c].at[k], ss5.at[c, 0], rs5.at[c, k], nz + k).wait_recv()

    def direct(c):
        value = jnp.concatenate([part[c][a][:t, :] for a in range(2)], axis=0)
        if c == 0:
            power = power_of(value[:, :width])
            powers[sub:] = power
        else:
            power = powers[sub:]
        code = coded(value, power)
        for a in range(2):
            s5[c][a] = code[a * t:(a + 1) * t, :].astype(jnp.int16)
            c5(c, a).start()

    def send_same(c, first):
        for d in range(first, half):
            @pl.when(d != spot)
            def _():
                c3(c, tier * half + d).start()

    def send_other(c):
        for d in range(half):
            c3(c, other_tier(d)).start()

    @pl.when(tier == 1)
    def _():
        pl.semaphore_wait(barrier, nz + 1)
        for d in range(half):
            greet(late_sem, device(other_tier(d)))

    turn()
    compute(0)

    @pl.when(tier == 0)
    def _():
        pl.semaphore_wait(barrier, half)


    @pl.when(tier == 1)
    def _():
        direct(0)

    c1(0).start()
    for c in range(chunks):
        if c + 1 < chunks:
            compute(c + 1)

            @pl.when(tier == 1)
            def _():
                direct(c + 1)

            c1(c + 1).start()
        encode(c)

        @pl.when(tier == 0)
        def _():
            send_same(c, 0)

        @pl.when(tier == 1)
        def _():
            for d in range(1, half):
                c3(c, d).start()
            if c + 1 == chunks:
                for k in range(chunks):
                    send_same(k, 0)

    @pl.when(tier == 0)
    def _():
        pl.semaphore_wait(late_sem, half)
        for c in range(chunks):
            send_other(c)

    others = [lax.rem(z + d, nz) for d in range(1, nz)]

    def number(code):
        return code.astype(jnp.int32).astype(jnp.float32)

    def finish(chips, cores):
        waits = [(r3, chip, r3_wait) for chip in chips] + [(r5, k, r5_wait) for k in range(cores)]
        scales = []
        for c in range(chunks):
            lo, hi = splits[c]
            cols = (hi - lo) * width
            ats = [(at, min(at + LANES, cols)) for at in range(0, cols, LANES)]
            totals = [own[c][z, :, at:end] for at, end in ats]
            for group in ((waits[:-2], waits[-2:]) if c + 1 == chunks else (waits,)):
                for _, src, wait in group:
                    wait(c, src)
                if c == 0:
                    scales = [jnp.exp2(number(r[c][src, :, cols:cols + LANES]) * (-1.0 / 256.0)) for r, src, _ in group]
                used = scales[-2:] if len(group) == 2 else scales[:len(group)]
                for i, (at, end) in enumerate(ats):
                    for (r, src, _), scale in zip(group, used):
                        totals[i] = totals[i] + number(r[c][src, :, at:end]) * scale[:, :end - at]
            for (at, end), total in zip(ats, totals):
                for s in range(lo + at // width, lo + end // width):
                    o_ref[s * t:(s + 1) * t, :] = total[:, (s - lo) * width - at:(s - lo + 1) * width - at]

    @pl.when(z == 0)
    def _():
        finish(list(range(1, half)), nz)

    @pl.when(z != 0)
    def _():
        finish(others, 0)

    for c in range(chunks):
        c1(c).wait_send()

    @pl.when(tier == 0)
    def _():
        for c in range(chunks):
            for chip in others:
                c3(c, chip).wait_send()

    @pl.when(tier == 1)
    def _():
        for c in range(chunks):
            for d in range(1, half):
                c3(c, d).wait_send()
                c3(c, same_tier(d)).wait_send()
            for side in range(2):
                c5(c, side).wait_send()


def unfold(t, v_ref, o_ref, lined):
    width = v_ref.shape[1]
    far = width // 2
    value = jnp.concatenate([v_ref[...], jnp.zeros((width * t - v_ref.shape[0], width), jnp.float32)], axis=0)
    lane = lax.broadcasted_iota(jnp.int32, value.shape, 1)
    step = 1
    while step < width:
        value = jnp.where((lane & step) != 0, jnp.roll(value, step * t, axis=0), value)
        step *= 2
    lined[...] = value
    row = lax.broadcasted_iota(jnp.int32, (width, width), 0)
    col = lax.broadcasted_iota(jnp.int32, (width, width), 1)
    near = within(row - col + width, width) <= far
    for q in range(t):
        at = pl.ds(q, width, stride=t)
        below = lined[at, :]
        lined[at, :] = jnp.where(near, below, below.T)
    per = LANES // width
    for m in range(width // per):
        o_ref[:, m * LANES:(m + 1) * LANES] = jnp.concatenate(
            [lined[(m * per + i) * t:(m * per + i + 1) * t, :] for i in range(per)], axis=1)


def per_device(row_leaves, covariates, query_leaves, leaf_sizes):
    n = lax.axis_size("rows")
    trees, rows = row_leaves.shape
    width = covariates.shape[0]
    queries = query_leaves.shape[1]
    t = queries // n
    nz = n // 2
    sub = nz * t
    cols = [(hi - lo) * width for lo, hi in splits_of(width)]
    chunks = len(cols)
    vmem = pl.BlockSpec(memory_space=pltpu.VMEM)
    f32 = jnp.float32
    i16 = jnp.int16
    dma = pltpu.SemaphoreType.DMA
    folded = pl.pallas_call(
        functools.partial(kernel, n),
        out_shape=pltpu.VMEM(((width // 2 + 1) * t, width), f32),
        in_specs=[pl.BlockSpec(memory_space=pltpu.HBM)] * 4,
        out_specs=vmem,
        scratch_shapes=[
            pltpu.VMEM(row_leaves.shape, jnp.int32),
            pltpu.VMEM(covariates.shape, jnp.bfloat16),
            pltpu.VMEM(query_leaves.shape, jnp.int32),
            pltpu.VMEM(leaf_sizes.shape, jnp.int32),
            pltpu.VMEM((TURNS, width + width // 2, rows), jnp.bfloat16),
            pltpu.VMEM((trees, queries, STEP), i16),
            pltpu.VMEM((trees, queries, STEP), i16),
            pltpu.VMEM((queries, rows), jnp.bfloat16),
            pltpu.VMEM((queries, queries), jnp.bfloat16),
            pltpu.VMEM((trees, trees * LANES), jnp.bfloat16),
            pltpu.VMEM((sub + 2 * t, LANES), f32),
            pltpu.SemaphoreType.REGULAR,
            dma((3,)), dma((rows // (PIECES * STEP),)),
            dma((chunks,)), dma((chunks,)),
            dma((chunks, nz)), dma((chunks, nz)),
            dma((chunks, 2)), dma((chunks, nz)),
            *[pltpu.VMEM((2, sub, c), f32) for c in cols],
            *[pltpu.VMEM((nz, t, c), f32) for c in cols],
            *[pltpu.VMEM((nz, t, coded_width(c)), i16) for c in cols],
            *[pltpu.VMEM((sub, c), f32) for c in cols],
            *[pltpu.VMEM((nz, t, coded_width(c)), i16) for c in cols],
            *[pltpu.VMEM((2, t, coded_width(c)), i16) for c in cols],
            *[pltpu.VMEM((nz, t, coded_width(c)), i16) for c in cols],
        ],
        compiler_params=pltpu.CompilerParams(collective_id=0, has_side_effects=True,
                                             vmem_limit_bytes=56 << 20),
    )(row_leaves, covariates, query_leaves, leaf_sizes)
    return pl.pallas_call(
        functools.partial(unfold, t),
        out_shape=jax.ShapeDtypeStruct((t, width * width), f32),
        in_specs=[vmem],
        out_specs=vmem,
        scratch_shapes=[pltpu.VMEM((width * t, width), f32)],
        compiler_params=pltpu.CompilerParams(vmem_limit_bytes=16 << 20),
    )(folded)


def solution(mesh):
    return jax.shard_map(
        per_device,
        mesh=mesh,
        in_specs=(
            P(None, ("groups", "rows")),
            P(None, ("groups", "rows")),
            P(None, "groups"),
            P("groups", None),
        ),
        out_specs=P(("groups", "rows"), None),
        check_vma=False,
    )
```
